32 devices in a mesh: grp: 2 (over y), ex: 4 (over z), col: 4 (over x, core).
Axes of the slice: x: 2, y: 2, z: 4, core: 2. Of those that a mesh axis runs over, the one named last changes fastest.
Arguments:
- hidden_input: bfloat16 [8, 2, 256, 5120], P(('grp', 'ex'), None, None, 'col'), parts along dimension 0, may hold values from -6 to 6
- output_gradient: bfloat16 [8, 2, 256, 5120], P(('grp', 'ex'), None, None, 'col'), parts along dimension 0, may hold values from -11 to 11
- lengths: int32 [8], P(('grp', 'ex')), parts along dimension 0, may hold values from 64 to 256
- adapter_down: bfloat16 [2, 128, 5120], P(None, None, 'col'), may hold values from -0.078125 to 0.078125
- adapter_up: bfloat16 [2, 5120, 128], P(None, 'col'), may hold values from -0.078125 to 0.078125
- left_sign_words: int32 [2, 2, 32, 5120], P(None, None, None, 'col'), may hold values from 0 to 65535
- right_sign_words: int32 [2, 2, 128, 4], replicated, may hold values from 0 to 1
- targets: float32 [512, 8192], P(('grp', 'ex'), 'col'), parts along dimension 0, may hold values from -40 to 40
Outputs:
- gradient_features: float32 [8, 8192], P(('grp', 'ex'), 'col'), parts along dimension 0
- scores: float32 [8, 256], P(('grp', 'ex'), 'col'), parts along dimension 0
The draws below stay inside these ranges and needn't reach their ends.
There are 2 independent parts, one for each index of `grp`. The reference program is written for one: setup_inputs(seed, part) draws one part's arguments, and reference() takes and returns one part's arrays. A program takes and returns all parts, laid end to end along the dimension named above; an argument that names none is the same for every part. Nothing has to cross between parts.
Inputs may be any that keep to these rules, and one draw needn't show every extreme that they name: `left_sign_words`: each word holds 16 independent bits.
All inputs are finite; a program needn't handle non-finite values.
Results may differ from the reference program's by a relative error of at most 0.0003.
Values sent between devices are 32-bit elements; how exact they have to be, the bound alone decides.
No kernel may reach another device: no remote copies, remote signals or barrier semaphores. Data moves between devices by JAX's collectives and lax.ppermute only.
A program may use at most 64 MiB of HBM per device.

```python
import math
import jax
import jax.numpy as jnp
from jax import lax

MODEL_WIDTH = 5120
ADAPTER_RANK = 128
SEQ = 256
ADAPTED_LAYERS = 2
K_LEFT = 512
M_RIGHT = 4
TARGETS = 256
CANDS = 4
COLS = 8192


def draw_output_gradient(key, part):
    shape_all = (CANDS, ADAPTED_LAYERS, SEQ, MODEL_WIDTH)
    levels = jnp.arange(ADAPTED_LAYERS, dtype=jnp.float32) / max(ADAPTED_LAYERS - 1, 1)
    values = jnp.clip(jax.random.normal(key, shape_all, jnp.float32), -6.0, 6.0)
    scales = 3.0 ** (0.5 * levels)
    return (values * scales[None, :, None, None]).astype(jnp.bfloat16)


def draw_targets(key, part):
    column_pos = jnp.arange(COLS, dtype=jnp.float32) / (COLS - 1)
    values = jnp.clip(jax.random.normal(key, (TARGETS, COLS), jnp.float32), -6.0, 6.0)
    return values * (3.0 ** (0.5 * column_pos))[None, :]


def with_ends(values, rng, least, top_value):
    longest = values.shape.index(max(values.shape))
    spots = []
    for shift in (0, 1):
        where = [jax.random.randint(jax.random.fold_in(rng, axis), (), 0, length) for axis, length in enumerate(values.shape)]
        where[longest] = (where[longest] + shift) % values.shape[longest]
        spots.append(tuple(where))
    return values.at[spots[0]].set(least).at[spots[1]].set(top_value)


def level_of(stream_key, dims, shards, low, largest):
    gain, own = 1.0, jax.random.fold_in(stream_key, 6)
    for axis_at, blocks in shards:
        heights = jnp.exp(jax.random.uniform(jax.random.fold_in(own, axis_at), (blocks,), jnp.float32, low / len(shards), largest / len(shards)))
        gain = gain * jnp.repeat(heights, dims[axis_at] // blocks).reshape([-1 if axis == axis_at else 1 for axis in range(len(dims))])
    return gain


def gaussian(rng, shape, spread, bound, cuts=(), held_as=jnp.bfloat16):
    gain = level_of(rng, shape, cuts, -0.22, 0.18) if cuts else 1.0
    result = jax.random.normal(rng, shape, jnp.float32) * spread * gain
    return jnp.minimum(jnp.maximum(result, -bound), bound).astype(held_as)


def setup_inputs(seed: int = 0, part: int = 0) -> dict:
    splits = jax.random.split(jax.random.key(seed), 9)
    part_splits = jax.random.split(jax.random.fold_in(splits[8], part), 9)
    hidden_input = gaussian(part_splits[0], (CANDS, ADAPTED_LAYERS, SEQ, MODEL_WIDTH), 1.0, 6.0, ((0, 4), (3, 4)))
    output_gradient = draw_output_gradient(jax.random.fold_in(jax.random.fold_in(splits[8], part), 71), part)
    lengths = with_ends(jax.random.randint(part_splits[2], (CANDS,), SEQ // 4, SEQ + 1), jax.random.fold_in(part_splits[2], 1), SEQ // 4, SEQ).astype(jnp.int32)
    adapter_down = gaussian(splits[3], (ADAPTED_LAYERS, ADAPTER_RANK, MODEL_WIDTH), MODEL_WIDTH ** -0.5, 0.078125, ((2, 4),))
    adapter_up = gaussian(splits[4], (ADAPTED_LAYERS, MODEL_WIDTH, ADAPTER_RANK), MODEL_WIDTH ** -0.5, 0.078125, ((1, 4),))
    left_sign_words = with_ends(jax.random.randint(splits[5], (ADAPTED_LAYERS, 2, K_LEFT // 16, MODEL_WIDTH), 0, 65536), jax.random.fold_in(splits[5], 1), 0, 65535).astype(jnp.int32)
    right_sign_words = with_ends(jax.random.randint(splits[6], (ADAPTED_LAYERS, 2, ADAPTER_RANK, M_RIGHT), 0, 2), jax.random.fold_in(splits[6], 1), 0, 1).astype(jnp.int32)
    targets = draw_targets(jax.random.fold_in(jax.random.fold_in(splits[8], part), 71), part)
    return {"hidden_input": hidden_input, "output_gradient": output_gradient, "lengths": lengths, "adapter_down": adapter_down, "adapter_up": adapter_up, "left_sign_words": left_sign_words, "right_sign_words": right_sign_words, "targets": targets}


epsilon = 1e-06
highest_precision = lax.Precision.HIGHEST

def unpack(packed):
    shifts = jnp.arange(16, dtype=jnp.int32)
    bit_values = jnp.right_shift(packed[..., :, None, :], shifts[:, None]) & 1
    shape_out = packed.shape[:-2] + (packed.shape[-2] * 16, packed.shape[-1])
    return (2 * bit_values - 1).reshape(shape_out)

def reference(hidden_input, output_gradient, lengths, adapter_down, adapter_up, left_sign_words, right_sign_words, targets):
    positions = jnp.arange(SEQ, dtype=jnp.int32)
    token_weights = jnp.where(positions[None, :] < lengths[:, None], 1.0, 0.0).astype(jnp.float32) / lengths[:, None].astype(jnp.float32)
    left_signs = unpack(left_sign_words).astype(jnp.float32)
    right_signs = (2 * right_sign_words - 1).astype(jnp.float32)
    blocks = []
    for index_of_layer in range(ADAPTED_LAYERS):
        input_rows = hidden_input[:, index_of_layer].astype(jnp.float32)
        gradient_value = output_gradient[:, index_of_layer].astype(jnp.float32)
        shrunk_input = jnp.einsum('aom,cm->aoc', input_rows, adapter_down[index_of_layer].astype(jnp.float32), precision=highest_precision)
        shrunk_gradient = jnp.einsum('wvl,lz->wvz', gradient_value, adapter_up[index_of_layer].astype(jnp.float32), precision=highest_precision)
        mixed_b = jnp.einsum('esr,rm->esm', shrunk_input, right_signs[index_of_layer, 0], precision=highest_precision) * token_weights[:, :, None]
        mixed_a = jnp.einsum('esr,rm->esm', shrunk_gradient, right_signs[index_of_layer, 1], precision=highest_precision) * token_weights[:, :, None]
        signed_grad = jnp.einsum('esd,kd->esk', gradient_value, left_signs[index_of_layer, 0], precision=highest_precision)
        signed_input = jnp.einsum('esd,kd->esk', input_rows, left_signs[index_of_layer, 1], precision=highest_precision)
        block_b = jnp.einsum('esm,esk->emk', mixed_b, signed_grad, precision=highest_precision)
        block_a = jnp.einsum('esm,esk->emk', mixed_a, signed_input, precision=highest_precision)
        blocks.append(jnp.stack([block_b, block_a], axis=1))
    sketch = jnp.stack(blocks, axis=1).reshape(CANDS, COLS)
    cand_squares = lax.optimization_barrier(jnp.sum(sketch * sketch, axis=1))
    gradient_features = sketch * lax.rsqrt(cand_squares / COLS + epsilon)[:, None]
    target_squares = lax.optimization_barrier(jnp.sum(targets * targets, axis=1))
    target_units = targets * lax.rsqrt(target_squares / COLS + epsilon)[:, None]
    scores = jnp.dot(gradient_features, target_units.T, precision=highest_precision) / math.sqrt(COLS)
    return (gradient_features, scores)
```

```python
import functools
import math

import jax
import jax.numpy as jnp
from jax import lax
from jax.experimental import pallas as pl
from jax.experimental.pallas import tpu as pltpu
from jax.sharding import PartitionSpec as P

epsilon = 1e-06
WORD = 16
f32, bf16 = jnp.float32, jnp.bfloat16
MIB = 1 << 20


def contract_last(a, b):
    return lax.dot_general(a, b, (((1,), (1,)), ((), ())), preferred_element_type=f32)


def halves(x):
    high = x.astype(bf16)
    return high, (x - high.astype(f32)).astype(bf16)


def partner(i, step, count):
    return i ^ step if count & (count - 1) == 0 else (i + step) % count


def shift(x, axis, count, step):
    return lax.ppermute(x, axis, [(i, partner(i, step, count)) for i in range(count)])


VMEM = pl.BlockSpec(memory_space=pltpu.VMEM)
SMEM = pl.BlockSpec(memory_space=pltpu.SMEM)
ANY = pl.BlockSpec(memory_space=pl.ANY)


def mix_kernel(right, hidden, grad, down, up, out, hid_buf, grad_buf, down_buf, up_buf, sems):
    layers = hidden.shape[1]
    copies = []
    for l in range(layers):
        group = []
        for k, (src, buf) in enumerate(
            (
                (down.at[l], down_buf.at[l]),
                (hidden.at[0, l], hid_buf.at[l]),
                (up.at[l], up_buf.at[l]),
                (grad.at[0, l], grad_buf.at[l]),
            )
        ):
            copy = pltpu.make_async_copy(src, buf, sems.at[l, k])
            copy.start()
            group.append(copy)
        copies.append(group)
    for l in range(layers):
        signs = (2 * right[l] - 1).astype(f32).astype(bf16)
        for j, (adapter, rows) in enumerate(((down_buf, hid_buf), (up_buf, grad_buf))):
            copies[l][2 * j].wait()
            if j == 0:
                mixed = jnp.dot(signs[j], adapter[l], preferred_element_type=f32)
            else:
                mixed = contract_last(signs[j], adapter[l])
            copies[l][2 * j + 1].wait()
            m = mixed.shape[0]
            both = contract_last(jnp.concatenate(halves(mixed), axis=0), rows[l])
            base = (2 * l + j) * m
            out[base : base + m, :] = both[:m] + both[m:]


def sign_kernel(words, hidden, grad, targets, high, low, target_high, target_low, squares,
                hid_buf, grad_buf, signs, sems):
    layers = hidden.shape[1]
    copies = []
    for l in range(layers):
        group = []
        for k, (src, buf) in enumerate(
            ((grad.at[0, l], grad_buf.at[l]), (hidden.at[0, l], hid_buf.at[l]))
        ):
            copy = pltpu.make_async_copy(src, buf, sems.at[l, k])
            copy.start()
            group.append(copy)
        copies.append(group)
    t = targets[...]
    target_high[...], target_low[...] = halves(t)
    squares[...] = jnp.sum(t * t, axis=1, keepdims=True)
    for l in range(layers):
        for j, rows in enumerate((grad_buf, hid_buf)):
            packed = words[l, j]
            w, d = packed.shape
            planes = [
                jnp.where((packed & (1 << b)) != 0, 1.0, -1.0).astype(f32)[:, None, :]
                for b in range(WORD)
            ]
            signs[...] = jnp.concatenate(planes, axis=1).reshape(w * WORD, d).astype(bf16)
            copies[l][j].wait()
            signed = contract_last(signs[...], rows[l])
            high[l, j], low[l, j] = halves(signed)


def sketch_kernel(cols, length, own, *refs):
    others, (high, low), outs, table = refs[: cols - 1], refs[cols - 1 : cols + 1], refs[cols + 1 : -1], refs[-1]
    me = lax.axis_index("col")
    mixed = own[...]
    for other in others:
        mixed = mixed + other[...]
    positions = lax.broadcasted_iota(jnp.int32, (1, mixed.shape[1]), 1)
    n = length[0]
    weights = jnp.where(positions < n, 1.0 / n.astype(f32), 0.0)
    mixed = mixed * weights
    layers, sides, k = high.shape[:3]
    m = mixed.shape[0] // (layers * sides)
    for l in range(layers):
        for j in range(sides):
            base = (2 * l + j) * m
            pair = jnp.concatenate(halves(mixed[base : base + m]), axis=0)
            both = contract_last(pair, high[l, j]) + contract_last(pair, low[l, j])
            rows = both[:m] + both[m:]
            for i in range(m):
                at = (base + i) * k
                block, within = divmod(at, table.shape[1])
                table[block : block + 1, within : within + k] = rows[i : i + 1]
    for step, out in enumerate(outs):
        to = partner(me, step, cols)
        out[...] = table[pl.ds(to, 1), :]


def sum_kernel(*refs):
    total = refs[0][...]
    for ref in refs[1:-1]:
        total = total + ref[...]
    refs[-1][...] = total


def score_kernel(exs, *refs):
    rows = jnp.concatenate([r[...] for r in refs[:exs]], axis=0)
    target_high, target_low, squares, out = refs[exs:]
    pair = jnp.concatenate(halves(rows), axis=0)
    both = contract_last(pair, target_high[...]) + contract_last(pair, target_low[...])
    count = target_high.shape[0]
    out[...] = jnp.zeros_like(out)
    out[0:exs, 0:count] = both[:exs] + both[exs:]
    out[0:exs, count : 2 * count] = jnp.broadcast_to(
        jnp.transpose(squares[...]), (exs, count)
    )
    out[exs : 2 * exs, :] = jnp.broadcast_to(
        jnp.sum(rows * rows, axis=1, keepdims=True), (exs, out.shape[1])
    )


def on_device(
    hidden_input,
    output_gradient,
    lengths,
    adapter_down,
    adapter_up,
    left_sign_words,
    right_sign_words,
    targets,
    *,
    exs,
    cols,
):
    _, layers, seq, width = hidden_input.shape
    m = right_sign_words.shape[3]
    rank = adapter_down.shape[1]
    k_left = left_sign_words.shape[2] * WORD
    count, own_cols = targets.shape
    all_cols = own_cols * cols
    params = functools.partial(pltpu.CompilerParams)
    right = jnp.swapaxes(right_sign_words, 2, 3)
    mixed = pl.pallas_call(
        mix_kernel,
        out_shape=jax.ShapeDtypeStruct((layers * 2 * m, seq), f32),
        in_specs=[VMEM, ANY, ANY, ANY, ANY],
        out_specs=VMEM,
        scratch_shapes=[
            pltpu.VMEM((layers, seq, width), bf16),
            pltpu.VMEM((layers, seq, width), bf16),
            pltpu.VMEM((layers, rank, width), bf16),
            pltpu.VMEM((layers, width, rank), bf16),
            pltpu.SemaphoreType.DMA((layers, 4)),
        ],
        compiler_params=params(vmem_limit_bytes=16 * MIB),
        name="mix",
    )(right, hidden_input, output_gradient, adapter_down, adapter_up)
    others = [shift(mixed, "col", cols, s) for s in range(1, cols)]
    signed = jax.ShapeDtypeStruct((layers, 2, k_left, seq), bf16)
    high, low, target_high, target_low, squares = pl.pallas_call(
        sign_kernel,
        out_shape=[
            signed,
            signed,
            jax.ShapeDtypeStruct(targets.shape, bf16),
            jax.ShapeDtypeStruct(targets.shape, bf16),
            jax.ShapeDtypeStruct((count, 1), f32),
        ],
        in_specs=[VMEM, ANY, ANY, VMEM],
        out_specs=[VMEM] * 5,
        scratch_shapes=[
            pltpu.VMEM((layers, seq, width), bf16),
            pltpu.VMEM((layers, seq, width), bf16),
            pltpu.VMEM((k_left, width), bf16),
            pltpu.SemaphoreType.DMA((layers, 2)),
        ],
        compiler_params=params(vmem_limit_bytes=24 * MIB),
        cost_estimate=pl.CostEstimate(
            flops=4 * layers * k_left * seq * width, bytes_accessed=4 * MIB, transcendentals=0
        ),
        name="sign",
    )(left_sign_words, hidden_input, output_gradient, targets)
    block = jax.ShapeDtypeStruct((1, own_cols), f32)
    blocks = pl.pallas_call(
        functools.partial(sketch_kernel, cols),
        out_shape=[block] * cols,
        in_specs=[SMEM] + [VMEM] * (cols + 2),
        out_specs=[VMEM] * cols,
        scratch_shapes=[pltpu.VMEM((cols, own_cols), f32)],
        compiler_params=params(vmem_limit_bytes=8 * MIB),
        name="sketch",
    )(lengths, mixed, *others, high, low)
    received = [shift(b, "col", cols, s) for s, b in enumerate(blocks) if s]
    own = pl.pallas_call(
        sum_kernel,
        out_shape=block,
        in_specs=[VMEM] * cols,
        out_specs=VMEM,
        compiler_params=params(vmem_limit_bytes=2 * MIB),
        name="own",
    )(blocks[0], *received)
    candidates = [own] + [shift(own, "ex", exs, s) for s in range(1, exs)]
    lanes = -(-2 * count // 128) * 128
    packed = pl.pallas_call(
        functools.partial(score_kernel, exs),
        out_shape=jax.ShapeDtypeStruct((2 * exs, lanes), f32),
        in_specs=[VMEM] * (exs + 3),
        out_specs=VMEM,
        compiler_params=params(vmem_limit_bytes=8 * MIB),
        name="score",
    )(*candidates, target_high, target_low, squares)
    me_ex = lax.axis_index("ex")
    order = jnp.stack([partner(me_ex, s, exs) if exs & (exs - 1) == 0 else (me_ex - s) % exs for s in range(exs)])
    per = exs // cols
    rows = jnp.stack([packed[:exs], packed[exs:]], axis=1)
    rows = jnp.zeros_like(rows).at[order].set(rows)
    grid = jnp.zeros((exs, cols) + rows.shape[1:], f32)
    grid = grid.at[:, me_ex // per].set(rows)
    back = lax.all_to_all(
        grid.reshape((exs * cols,) + rows.shape[1:]), ("ex", "col"), 0, 0, tiled=True
    ).reshape((exs, cols) + rows.shape[1:])
    me_col = lax.axis_index("col")
    mine = lax.dynamic_slice_in_dim(back, me_col * per, per, axis=0).sum(axis=1)
    raw = mine[:, 0, :count].reshape(1, -1)
    target_squares = mine[:, 0, count : 2 * count].reshape(1, -1)
    square = mine[0, 1, 0]
    scale = lax.rsqrt(square / all_cols + epsilon)
    features = own * scale
    scores = raw * scale * lax.rsqrt(target_squares / all_cols + epsilon) / math.sqrt(all_cols)
    return features, scores


def solution(mesh):
    body = functools.partial(on_device, exs=mesh.shape["ex"], cols=mesh.shape["col"])
    return jax.shard_map(
        body,
        mesh=mesh,
        in_specs=(
            P(("grp", "ex"), None, None, "col"),
            P(("grp", "ex"), None, None, "col"),
            P(("grp", "ex")),
            P(None, None, "col"),
            P(None, "col", None),
            P(None, None, None, "col"),
            P(),
            P(("grp", "ex"), "col"),
        ),
        out_specs=(P(("grp", "ex"), "col"), P(("grp", "ex"), "col")),
        check_vma=False,
    )
```

```python
import functools
import math

import jax
import jax.numpy as jnp
from jax import lax
from jax.experimental import pallas as pl
from jax.experimental.pallas import tpu as pltpu
from jax.sharding import PartitionSpec as P

epsilon = 1e-06
WORD = 16
LANES = 128
IN_FLIGHT = 2
f32, bf16 = jnp.float32, jnp.bfloat16
MIB = 1 << 20

VMEM = pl.BlockSpec(memory_space=pltpu.VMEM)
SMEM = pl.BlockSpec(memory_space=pltpu.SMEM)
HBM = pl.BlockSpec(memory_space=pltpu.HBM)


def contract_last(a, b):
    return lax.dot_general(a, b, (((1,), (1,)), ((), ())), preferred_element_type=f32)


def halves(x):
    high = x.astype(bf16)
    return high, (x - high.astype(f32)).astype(bf16)


def partner(i, step, count):
    return i ^ step if count & (count - 1) == 0 else (i + step) % count


def shift(x, axis, count, step):
    return lax.ppermute(x, axis, [(i, partner(i, step, count)) for i in range(count)])


def in_hbm(*arrays):
    return [pltpu.with_memory_space_constraint(x, pltpu.HBM) for x in arrays]


def mix_kernel(right, hidden, grad, down, up, out, hid_out, grad_out, right_buf, down_buf, up_buf, sems):
    layers = hidden.shape[1]
    groups = []
    for l in range(layers):
        for j, (adapter, adapter_to, rows, rows_to) in enumerate(
            ((down, down_buf, hidden, hid_out), (up, up_buf, grad, grad_out))
        ):
            at = 2 * l + j
            groups.append(
                (
                    pltpu.make_async_copy(adapter.at[l], adapter_to.at[l], sems.at[at, 0]),
                    pltpu.make_async_copy(rows.at[0, l], rows_to.at[0, l], sems.at[at, 1]),
                )
            )
    signs_copy = pltpu.make_async_copy(right, right_buf, sems.at[2 * layers, 0])
    signs_copy.start()
    for group in groups[:IN_FLIGHT]:
        for copy in group:
            copy.start()
    signs_copy.wait()
    for at, group in enumerate(groups):
        l, j = divmod(at, 2)
        signs = (2 * right_buf[l, j] - 1).astype(f32).astype(bf16)
        group[0].wait()
        if j == 0:
            mixed = jnp.dot(signs, down_buf[l], preferred_element_type=f32)
        else:
            mixed = contract_last(signs, up_buf[l])
        pair = jnp.concatenate(halves(mixed), axis=0)
        group[1].wait()
        for copy in groups[at + IN_FLIGHT] if at + IN_FLIGHT < len(groups) else ():
            copy.start()
        m = mixed.shape[0]
        both = contract_last(pair, (hid_out if j == 0 else grad_out)[0, l])
        out[at * m : (at + 1) * m, :] = both[:m] + both[m:]


def unpack(words, l, j, out):
    bits = 1 << lax.broadcasted_iota(jnp.int32, (WORD, 1), 0)
    width = words.shape[3]
    for w in range(words.shape[2]):
        word = jnp.broadcast_to(words[l, j, w : w + 1, :], (WORD, width))
        signs = jnp.where((word & bits) != 0, 1.0, -1.0)
        out[w * WORD : (w + 1) * WORD, :] = signs.astype(f32).astype(bf16)


def sign_kernel(words, hidden, grad, targets, high, low, target_high, target_low, squares, signs):
    t = targets[...]
    target_high[...], target_low[...] = halves(t)
    squares[...] = jnp.transpose(jnp.sum(t * t, axis=1, keepdims=True))
    items = [(l, j) for l in range(hidden.shape[1]) for j in range(2)]
    unpack(words, *items[0], signs.at[0])
    for i, (l, j) in enumerate(items):
        if i + 1 < len(items):
            unpack(words, *items[i + 1], signs.at[(i + 1) % 2])
        signed = contract_last(signs[i % 2], (grad if j == 0 else hidden)[0, l])
        high[l, j], low[l, j] = halves(signed)


def sketch_kernel(exs, cols, length, own, *refs):
    others, (high, low, out) = refs[: cols - 1], refs[cols - 1 :]
    mixed = own[...]
    for other in others:
        mixed = mixed + other[...]
    positions = lax.broadcasted_iota(jnp.int32, (1, mixed.shape[1]), 1)
    n = length[0]
    mixed = mixed * jnp.where(positions < n, 1.0 / n.astype(f32), 0.0)
    layers, sides, k = high.shape[:3]
    m = mixed.shape[0] // (layers * sides)
    pieces = []
    for l in range(layers):
        for j in range(sides):
            base = (2 * l + j) * m
            pair = jnp.concatenate(halves(mixed[base : base + m]), axis=0)
            both = contract_last(pair, high[l, j]) + contract_last(pair, low[l, j])
            both = both[:m] + both[m:]
            pieces += [both[:, q : q + LANES] for q in range(0, k, LANES)]
    per = len(pieces) // cols
    for i in range(cols):
        block = jnp.concatenate(pieces[i * per : (i + 1) * per], axis=0)
        for e in range(exs):
            out[e * cols + i] = block


def column_starts(m, k, count):
    per = k // LANES
    return [
        (r // (m * per)) * m * k + (r % m) * k + (r // m % per) * LANES for r in range(count)
    ]


def score_kernel(exs, cols, m, k, received, target_high, target_low, squares, own, out):
    x = received[...]
    x = x.reshape((exs, cols) + x.shape[1:])
    total = x[:, 0]
    for i in range(1, cols):
        total = total + x[:, i]
    starts = column_starts(m, k, total.shape[1])
    order = sorted(range(len(starts)), key=lambda r: starts[r])
    rows = jnp.concatenate([total[:, r, :] for r in order], axis=1)
    pair = jnp.concatenate(halves(rows), axis=0)
    both = contract_last(pair, target_high[...]) + contract_last(pair, target_low[...])
    count = target_high.shape[0]
    out[...] = jnp.zeros_like(out)
    out[0:exs, 0:count] = both[:exs] + both[exs:]
    out[0:exs, count : 2 * count] = jnp.broadcast_to(squares[...], (exs, count))
    out[exs : 2 * exs, :] = jnp.broadcast_to(
        jnp.sum(rows * rows, axis=1, keepdims=True), (exs, out.shape[1])
    )
    me = lax.axis_index("ex")
    mine = received[pl.ds(me * cols, cols)]
    total = mine[0]
    for i in range(1, cols):
        total = total + mine[i]
    own[...] = total


def send_kernel(exs, cols, a, b, *outs):
    me = lax.axis_index("col")
    for step, out in zip(range(0, exs, 2), outs):
        e = me ^ step
        out[...] = jnp.zeros_like(out)
        out[0:1] = a[pl.ds(e, 1), :] + b[pl.ds(e, 1), :]
        out[1:2] = a[pl.ds(exs + e, 1), :] + b[pl.ds(exs + e, 1), :]


def last_kernel(all_cols, m, k, own, *refs):
    parts, (features, scores) = refs[:-2], refs[-2:]
    total = parts[0][...]
    for part in parts[1:]:
        total = total + part[...]
    count = scores.shape[1]
    scale = lax.rsqrt(total[1:2, 0:1] / all_cols + epsilon)
    target_scale = lax.rsqrt(total[0:1, count : 2 * count] / all_cols + epsilon)
    scores[...] = total[0:1, 0:count] * scale * target_scale / math.sqrt(all_cols)
    block = own[...] * scale
    for r, at in enumerate(column_starts(m, k, block.shape[0])):
        features[:, at : at + LANES] = block[r : r + 1]


def call(kernel, out_shape, in_specs, name, limit, scratch=(), flops=0, moved=0):
    single = not isinstance(out_shape, list)
    return pl.pallas_call(
        kernel,
        out_shape=out_shape,
        in_specs=in_specs,
        out_specs=VMEM if single else [VMEM] * len(out_shape),
        scratch_shapes=scratch,
        compiler_params=pltpu.CompilerParams(vmem_limit_bytes=limit * MIB),
        cost_estimate=pl.CostEstimate(flops=flops, bytes_accessed=moved, transcendentals=0),
        name=name,
    )


def on_device(
    hidden_input,
    output_gradient,
    lengths,
    adapter_down,
    adapter_up,
    left_sign_words,
    right_sign_words,
    targets,
    *,
    exs,
    cols,
):
    _, layers, seq, width = hidden_input.shape
    m = right_sign_words.shape[3]
    rank = adapter_down.shape[1]
    k = left_sign_words.shape[2] * WORD
    count, own_cols = targets.shape
    all_cols = own_cols * cols
    right = jnp.swapaxes(right_sign_words, 2, 3)
    rows = jax.ShapeDtypeStruct(hidden_input.shape, bf16)
    mixed, hidden, grad = call(
        mix_kernel,
        [jax.ShapeDtypeStruct((layers * 2 * m, seq), f32), rows, rows],
        [HBM] * 5,
        "mix",
        8,
        [
            pltpu.VMEM(right.shape, jnp.int32),
            pltpu.VMEM((layers, rank, width), bf16),
            pltpu.VMEM((layers, width, rank), bf16),
            pltpu.SemaphoreType.DMA((2 * layers + 1, 2)),
        ],
        4 * layers * seq * width * rank,
        4 * MIB,
    )(*in_hbm(right, hidden_input, output_gradient, adapter_down, adapter_up))
    others = [shift(mixed, "col", cols, s) for s in range(1, cols)]
    signed = jax.ShapeDtypeStruct((layers, 2, k, seq), bf16)
    target_half = jax.ShapeDtypeStruct(targets.shape, bf16)
    high, low, target_high, target_low, squares = call(
        sign_kernel,
        [signed, signed, target_half, target_half, jax.ShapeDtypeStruct((1, count), f32)],
        [VMEM] * 4,
        "sign",
        8,
        [pltpu.VMEM((2, k, width), bf16)],
        4 * layers * k * seq * width,
        6 * MIB,
    )(left_sign_words, hidden, grad, targets)
    block = (own_cols // LANES, LANES)
    blocks = call(
        functools.partial(sketch_kernel, exs, cols),
        jax.ShapeDtypeStruct((exs * cols,) + block, f32),
        [SMEM] + [VMEM] * (cols + 2),
        "sketch",
        8,
    )(lengths, mixed, *others, high, low)
    received = lax.all_to_all(blocks, ("ex", "col"), 0, 0, tiled=True)
    lanes = -(-2 * count // LANES) * LANES
    own, packed = call(
        functools.partial(score_kernel, exs, cols, m, k),
        [jax.ShapeDtypeStruct(block, f32), jax.ShapeDtypeStruct((2 * exs, lanes), f32)],
        [VMEM] * 4,
        "score",
        16,
    )(received, target_high, target_low, squares)
    results = [
        jax.ShapeDtypeStruct((1, own_cols), f32),
        jax.ShapeDtypeStruct((1, count * exs // cols), f32),
    ]
    if exs == cols and exs % 2 == 0 and exs & (exs - 1) == 0:
        neighbour = shift(packed, "col", cols, 1)
        sent = call(
            functools.partial(send_kernel, exs, cols),
            [jax.ShapeDtypeStruct((8, lanes), f32)] * (exs // 2),
            [VMEM] * 2,
            "send",
            2,
        )(packed, neighbour)
        parts = [
            lax.ppermute(
                x,
                ("ex", "col"),
                [(a * cols + i, (i ^ step) * cols + a) for a in range(exs) for i in range(cols)],
            )
            for step, x in zip(range(0, exs, 2), sent)
        ]
        return tuple(
            call(
                functools.partial(last_kernel, all_cols, m, k),
                results,
                [VMEM] * (1 + len(parts)),
                "last",
                2,
            )(own, *parts)
        )
    per = exs // cols
    rows = jnp.stack([packed[:exs], packed[exs:]], axis=1)
    grid = jnp.zeros((exs, cols) + rows.shape[1:], f32)
    grid = grid.at[:, lax.axis_index("ex") // per].set(rows)
    back = lax.all_to_all(
        grid.reshape((exs * cols,) + rows.shape[1:]), ("ex", "col"), 0, 0, tiled=True
    ).reshape((exs, cols) + rows.shape[1:])
    mine = lax.dynamic_slice_in_dim(back, lax.axis_index("col") * per, per, axis=0).sum(axis=1)
    total = jnp.concatenate(
        [
            jnp.concatenate([mine[:, 0, :count].reshape(1, -1), mine[:, 0, count : 2 * count].reshape(1, -1)], axis=1),
            jnp.broadcast_to(mine[:1, 1, :1], (1, 2 * count * per)),
        ],
        axis=0,
    )
    return tuple(
        call(functools.partial(last_kernel, all_cols, m, k), results, [VMEM] * 2, "last", 2)(own, total)
    )


def solution(mesh):
    body = functools.partial(on_device, exs=mesh.shape["ex"], cols=mesh.shape["col"])
    return jax.shard_map(
        body,
        mesh=mesh,
        in_specs=(
            P(("grp", "ex"), None, None, "col"),
            P(("grp", "ex"), None, None, "col"),
            P(("grp", "ex")),
            P(None, None, "col"),
            P(None, "col", None),
            P(None, None, None, "col"),
            P(),
            P(("grp", "ex"), "col"),
        ),
        out_specs=(P(("grp", "ex"), "col"), P(("grp", "ex"), "col")),
        check_vma=False,
    )
```

```python
import functools
import math

import jax
import jax.numpy as jnp
from jax import lax
from jax.experimental import pallas as pl
from jax.experimental.pallas import tpu as pltpu
from jax.sharding import PartitionSpec as P

epsilon = 1e-06
WORD = 16
LANES = 128
f32, bf16 = jnp.float32, jnp.bfloat16
MIB = 1 << 20

VMEM = pl.BlockSpec(memory_space=pltpu.VMEM)
HBM = pl.BlockSpec(memory_space=pltpu.HBM)


def contract_last(a, b):
    return lax.dot_general(a, b, (((1,), (1,)), ((), ())), preferred_element_type=f32)


def halves(x):
    high = x.astype(bf16)
    return high, (x - high.astype(f32)).astype(bf16)


def partner(i, step, count):
    return i ^ step if count & (count - 1) == 0 else (i + step) % count


def shift(x, axis, count, step):
    return lax.ppermute(x, axis, [(i, partner(i, step, count)) for i in range(count)])


def in_hbm(*arrays):
    return [pltpu.with_memory_space_constraint(x, pltpu.HBM) for x in arrays]


def mix_kernel(
    right, hidden, grad, down, up, out, hid_out, grad_out, right_buf, down_buf, up_buf, sems
):
    layers = hidden.shape[1]
    sides = [(l, j) for l in range(layers) for j in range(2)]
    first = [(right, right_buf)]
    first += [((up if j else down).at[l], (up_buf if j else down_buf).at[l]) for l, j in sides]
    rows = [
        ((grad if j else hidden).at[0, l], (grad_out if j else hid_out).at[0, l]) for l, j in sides
    ]
    copies = [pltpu.make_async_copy(a, b, sems.at[i]) for i, (a, b) in enumerate(first + rows)]
    for copy in copies:
        copy.start()
    for copy in copies[: len(first)]:
        copy.wait()
    pairs = []
    for l, j in sides:
        signs = (2 * right_buf[l, j] - 1).astype(f32).astype(bf16)
        if j == 0:
            folded = jnp.dot(signs, down_buf[l], preferred_element_type=f32)
        else:
            folded = contract_last(signs, up_buf[l])
        pairs.append(jnp.concatenate(halves(folded), axis=0))
    for copy in copies[len(first) :]:
        copy.wait()
    for at, (l, j) in enumerate(sides):
        both = contract_last(pairs[at], (grad_out if j else hid_out)[0, l])
        m = both.shape[0] // 2
        out[at * m : (at + 1) * m, :] = both[:m] + both[m:]


def unpack(words, l, j, out):
    bits = 1 << lax.broadcasted_iota(jnp.int32, (WORD, 1), 0)
    width = words.shape[3]
    for w in range(words.shape[2]):
        word = jnp.broadcast_to(words[l, j, w : w + 1, :], (WORD, width))
        signs = jnp.where((word & bits) != 0, 1.0, -1.0)
        out[w * WORD : (w + 1) * WORD, :] = signs.astype(f32).astype(bf16)


def sign_kernel(words, hidden, grad, targets, high, low, target_high, target_low, squares, signs):
    t = targets[...]
    target_high[...], target_low[...] = halves(t)
    squares[...] = jnp.transpose(jnp.sum(t * t, axis=1, keepdims=True))
    items = [(l, j) for l in range(hidden.shape[1]) for j in range(2)]
    unpack(words, *items[0], signs.at[0])
    for i, (l, j) in enumerate(items):
        if i + 1 < len(items):
            unpack(words, *items[i + 1], signs.at[(i + 1) % 2])
        signed = contract_last(signs[i % 2], (grad if j == 0 else hidden)[0, l])
        high[l, j], low[l, j] = halves(signed)


def sketch_kernel(exs, cols, length, own, *refs):
    others, (high, low, out) = refs[: cols - 1], refs[cols - 1 :]
    mixed = own[...]
    for other in others:
        mixed = mixed + other[...]
    n = length[...]
    positions = lax.broadcasted_iota(jnp.int32, (1, mixed.shape[1]), 1)
    mixed = mixed * jnp.where(positions < n, 1.0 / n.astype(f32), 0.0)
    layers, sides, k = high.shape[:3]
    m = mixed.shape[0] // (layers * sides)
    pieces = []
    for l in range(layers):
        for j in range(sides):
            base = (2 * l + j) * m
            pair = jnp.concatenate(halves(mixed[base : base + m]), axis=0)
            both = contract_last(pair, high[l, j]) + contract_last(pair, low[l, j])
            both = both[:m] + both[m:]
            pieces += [both[:, q : q + LANES] for q in range(0, k, LANES)]
    per = len(pieces) // cols
    for i in range(cols):
        block = jnp.concatenate(pieces[i * per : (i + 1) * per], axis=0)
        for e in range(exs):
            out[e * cols + i] = block


def column_starts(m, k, count):
    per = k // LANES
    return [
        (r // (m * per)) * m * k + (r % m) * k + (r // m % per) * LANES for r in range(count)
    ]


def score_kernel(exs, cols, m, k, received, target_high, target_low, squares, own, out):
    x = received[...]
    x = x.reshape((exs, cols) + x.shape[1:])
    total = x[:, 0]
    for i in range(1, cols):
        total = total + x[:, i]
    starts = column_starts(m, k, total.shape[1])
    order = sorted(range(len(starts)), key=lambda r: starts[r])
    rows = jnp.concatenate([total[:, r, :] for r in order], axis=1)
    pair = jnp.concatenate(halves(rows), axis=0)
    both = contract_last(pair, target_high[...]) + contract_last(pair, target_low[...])
    count = target_high.shape[0]
    out[...] = jnp.zeros_like(out)
    out[0:exs, 0:count] = both[:exs] + both[exs:]
    out[0:exs, count : 2 * count] = jnp.broadcast_to(squares[...], (exs, count))
    out[exs : 2 * exs, :] = jnp.broadcast_to(
        jnp.sum(rows * rows, axis=1, keepdims=True), (exs, out.shape[1])
    )
    me = lax.axis_index("ex")
    mine = received[pl.ds(me * cols, cols)]
    total = mine[0]
    for i in range(1, cols):
        total = total + mine[i]
    own[...] = total


def send_kernel(exs, cols, a, b, *outs):
    me = lax.axis_index("col")
    for step, out in zip(range(0, exs, 2), outs):
        e = me ^ step
        out[...] = jnp.zeros_like(out)
        out[0:1] = a[pl.ds(e, 1), :] + b[pl.ds(e, 1), :]
        out[1:2] = a[pl.ds(exs + e, 1), :] + b[pl.ds(exs + e, 1), :]


def last_kernel(all_cols, m, k, own, *refs):
    parts, (features, scores) = refs[:-2], refs[-2:]
    total = parts[0][...]
    for part in parts[1:]:
        total = total + part[...]
    count = scores.shape[1]
    scale = lax.rsqrt(total[1:2, 0:1] / all_cols + epsilon)
    target_scale = lax.rsqrt(total[0:1, count : 2 * count] / all_cols + epsilon)
    scores[...] = total[0:1, 0:count] * scale * target_scale / math.sqrt(all_cols)
    block = own[...] * scale
    for r, at in enumerate(column_starts(m, k, block.shape[0])):
        features[:, at : at + LANES] = block[r : r + 1]


def call(kernel, out_shape, in_specs, name, limit, scratch=(), flops=0, moved=0):
    single = not isinstance(out_shape, list)
    return pl.pallas_call(
        kernel,
        out_shape=out_shape,
        in_specs=in_specs,
        out_specs=VMEM if single else [VMEM] * len(out_shape),
        scratch_shapes=scratch,
        compiler_params=pltpu.CompilerParams(vmem_limit_bytes=limit * MIB),
        cost_estimate=pl.CostEstimate(flops=flops, bytes_accessed=moved, transcendentals=0),
        name=name,
    )


def on_device(
    hidden_input,
    output_gradient,
    lengths,
    adapter_down,
    adapter_up,
    left_sign_words,
    right_sign_words,
    targets,
    *,
    exs,
    cols,
):
    _, layers, seq, width = hidden_input.shape
    m = right_sign_words.shape[3]
    rank = adapter_down.shape[1]
    k = left_sign_words.shape[2] * WORD
    count, own_cols = targets.shape
    all_cols = own_cols * cols
    right = jnp.swapaxes(right_sign_words, 2, 3)
    rows = jax.ShapeDtypeStruct(hidden_input.shape, bf16)
    mixed, hidden, grad = call(
        mix_kernel,
        [jax.ShapeDtypeStruct((layers * 2 * m, seq), f32), rows, rows],
        [HBM] * 5,
        "mix",
        8,
        [
            pltpu.VMEM(right.shape, jnp.int32),
            pltpu.VMEM((layers, rank, width), bf16),
            pltpu.VMEM((layers, width, rank), bf16),
            pltpu.SemaphoreType.DMA((4 * layers + 1,)),
        ],
        4 * layers * seq * width * rank,
        4 * MIB,
    )(*in_hbm(right, hidden_input, output_gradient, adapter_down, adapter_up))
    others = [shift(mixed, "col", cols, s) for s in range(1, cols)]
    signed = jax.ShapeDtypeStruct((layers, 2, k, seq), bf16)
    target_half = jax.ShapeDtypeStruct(targets.shape, bf16)
    high, low, target_high, target_low, squares = call(
        sign_kernel,
        [signed, signed, target_half, target_half, jax.ShapeDtypeStruct((1, count), f32)],
        [VMEM] * 4,
        "sign",
        8,
        [pltpu.VMEM((2, k, width), bf16)],
        4 * layers * k * seq * width,
        6 * MIB,
    )(left_sign_words, hidden, grad, targets)
    block = (own_cols // LANES, LANES)
    blocks = call(
        functools.partial(sketch_kernel, exs, cols),
        jax.ShapeDtypeStruct((exs * cols,) + block, f32),
        [VMEM] * (cols + 3),
        "sketch",
        8,
    )(lengths.reshape(1, 1), mixed, *others, high, low)
    received = lax.all_to_all(blocks, ("ex", "col"), 0, 0, tiled=True)
    lanes = -(-2 * count // LANES) * LANES
    own, packed = call(
        functools.partial(score_kernel, exs, cols, m, k),
        [jax.ShapeDtypeStruct(block, f32), jax.ShapeDtypeStruct((2 * exs, lanes), f32)],
        [VMEM] * 4,
        "score",
        16,
    )(received, target_high, target_low, squares)
    results = [
        jax.ShapeDtypeStruct((1, own_cols), f32),
        jax.ShapeDtypeStruct((1, count * exs // cols), f32),
    ]
    if exs == cols and exs % 2 == 0 and exs & (exs - 1) == 0:
        neighbour = shift(packed, "col", cols, 1)
        sent = call(
            functools.partial(send_kernel, exs, cols),
            [jax.ShapeDtypeStruct((8, lanes), f32)] * (exs // 2),
            [VMEM] * 2,
            "send",
            2,
        )(packed, neighbour)
        parts = [
            lax.ppermute(
                x,
                ("ex", "col"),
                [(a * cols + i, (i ^ step) * cols + a) for a in range(exs) for i in range(cols)],
            )
            for step, x in zip(range(0, exs, 2), sent)
        ]
        return tuple(
            call(
                functools.partial(last_kernel, all_cols, m, k),
                results,
                [VMEM] * (1 + len(parts)),
                "last",
                2,
            )(own, *parts)
        )
    per = exs // cols
    rows = jnp.stack([packed[:exs], packed[exs:]], axis=1)
    grid = jnp.zeros((exs, cols) + rows.shape[1:], f32)
    grid = grid.at[:, lax.axis_index("ex") // per].set(rows)
    back = lax.all_to_all(
        grid.reshape((exs * cols,) + rows.shape[1:]), ("ex", "col"), 0, 0, tiled=True
    ).reshape((exs, cols) + rows.shape[1:])
    mine = lax.dynamic_slice_in_dim(back, lax.axis_index("col") * per, per, axis=0).sum(axis=1)
    total = jnp.concatenate(
        [
            jnp.concatenate([mine[:, 0, :count].reshape(1, -1), mine[:, 0, count : 2 * count].reshape(1, -1)], axis=1),
            jnp.broadcast_to(mine[:1, 1, :1], (1, 2 * count * per)),
        ],
        axis=0,
    )
    return tuple(
        call(functools.partial(last_kernel, all_cols, m, k), results, [VMEM] * 2, "last", 2)(own, total)
    )


def solution(mesh):
    body = functools.partial(on_device, exs=mesh.shape["ex"], cols=mesh.shape["col"])
    return jax.shard_map(
        body,
        mesh=mesh,
        in_specs=(
            P(("grp", "ex"), None, None, "col"),
            P(("grp", "ex"), None, None, "col"),
            P(("grp", "ex")),
            P(None, None, "col"),
            P(None, "col", None),
            P(None, None, None, "col"),
            P(),
            P(("grp", "ex"), "col"),
        ),
        out_specs=(P(("grp", "ex"), "col"), P(("grp", "ex"), "col")),
        check_vma=False,
    )
```

```python
import functools
import math

import jax
import jax.numpy as jnp
from jax import lax
from jax.experimental import pallas as pl
from jax.experimental.pallas import tpu as pltpu
from jax.sharding import PartitionSpec as P

epsilon = 1e-06
WORD = 16
STEPS = (3, 2, 1)
LANES = 128
f32, bf16 = jnp.float32, jnp.bfloat16
MIB = 1 << 20

VMEM = pl.BlockSpec(memory_space=pltpu.VMEM)
HBM = pl.BlockSpec(memory_space=pltpu.HBM)


def contract_last(a, b):
    return lax.dot_general(a, b, (((1,), (1,)), ((), ())), preferred_element_type=f32)


def halves(x):
    high = x.astype(bf16)
    return high, (x - high.astype(f32)).astype(bf16)


def partner(i, step, count):
    return i ^ step if count & (count - 1) == 0 else (i + step) % count


def shift(x, axis, count, step):
    return lax.ppermute(x, axis, [(i, partner(i, step, count)) for i in range(count)])


def in_hbm(*arrays):
    return [pltpu.with_memory_space_constraint(x, pltpu.HBM) for x in arrays]


def mix_kernel(
    right, hidden, grad, down, up, out, hid_out, grad_out, right_buf, down_buf, up_buf, sems
):
    layers = hidden.shape[1]
    sides = [(l, j) for l in range(layers) for j in range(2)]
    first = [(right, right_buf)]
    first += [((up if j else down).at[l], (up_buf if j else down_buf).at[l]) for l, j in sides]
    rows = [
        ((grad if j else hidden).at[0, l], (grad_out if j else hid_out).at[0, l]) for l, j in sides
    ]
    copies = [pltpu.make_async_copy(a, b, sems.at[i]) for i, (a, b) in enumerate(first + rows)]
    for copy in copies:
        copy.start()
    for copy in copies[: len(first)]:
        copy.wait()
    pairs = []
    for l, j in sides:
        signs = (2 * right_buf[l, j] - 1).astype(f32).astype(bf16)
        if j == 0:
            folded = jnp.dot(signs, down_buf[l], preferred_element_type=f32)
        else:
            folded = contract_last(signs, up_buf[l])
        pairs.append(jnp.concatenate(halves(folded), axis=0))
    for copy in copies[len(first) :]:
        copy.wait()
    for at, (l, j) in enumerate(sides):
        both = contract_last(pairs[at], (grad_out if j else hid_out)[0, l])
        m = both.shape[0] // 2
        out[at * m : (at + 1) * m, :] = both[:m] + both[m:]


def unpack(words, l, j, out):
    bits = 1 << lax.broadcasted_iota(jnp.int32, (WORD, 1), 0)
    width = words.shape[3]
    for w in range(words.shape[2]):
        word = jnp.broadcast_to(words[l, j, w : w + 1, :], (WORD, width))
        signs = jnp.where((word & bits) != 0, 1.0, -1.0)
        out[w * WORD : (w + 1) * WORD, :] = signs.astype(f32).astype(bf16)


def split_kernel(targets, high, low, squares):
    t = targets[...]
    high[...], low[...] = halves(t)
    squares[...] = jnp.transpose(jnp.sum(t * t, axis=1, keepdims=True))


def sign_kernel(words, hidden, grad, high, low, signs):
    items = [(l, j) for l in range(hidden.shape[1]) for j in range(2)]
    unpack(words, *items[0], signs.at[0])
    for i, (l, j) in enumerate(items):
        if i + 1 < len(items):
            unpack(words, *items[i + 1], signs.at[(i + 1) % 2])
        signed = contract_last(signs[i % 2], (grad if j == 0 else hidden)[0, l])
        high[l, j], low[l, j] = halves(signed)


def sketch_blocks(cols, length, own, others, high, low):
    mixed = own[...]
    for other in others:
        mixed = mixed + other[...]
    n = length[...]
    positions = lax.broadcasted_iota(jnp.int32, (1, mixed.shape[1]), 1)
    mixed = mixed * jnp.where(positions < n, 1.0 / n.astype(f32), 0.0)
    layers, sides, k = high.shape[:3]
    m = mixed.shape[0] // (layers * sides)
    pieces = []
    for l in range(layers):
        for j in range(sides):
            base = (2 * l + j) * m
            pair = jnp.concatenate(halves(mixed[base : base + m]), axis=0)
            both = contract_last(pair, high[l, j]) + contract_last(pair, low[l, j])
            both = both[:m] + both[m:]
            pieces += [both[:, q : q + LANES] for q in range(0, k, LANES)]
    per = len(pieces) // cols
    return [jnp.concatenate(pieces[i * per : (i + 1) * per], axis=0) for i in range(cols)]


def spread_kernel(exs, cols, length, own, *refs):
    others, (high, low, out) = refs[: cols - 1], refs[cols - 1 :]
    for i, block in enumerate(sketch_blocks(cols, length, own, others, high, low)):
        for e in range(exs):
            out[e * cols + i] = block


def pair_kernel(cols, length, own, *refs):
    others, (high, low), outs, table = refs[: cols - 1], refs[cols - 1 : cols + 1], refs[cols + 1 : -1], refs[-1]
    for i, block in enumerate(sketch_blocks(cols, length, own, others, high, low)):
        table[i] = block
    me = lax.axis_index("col")
    for step, out in enumerate(outs):
        out[...] = table[partner(me, step, cols)]


def sum_kernel(*refs):
    total = refs[0][...]
    for ref in refs[1:-1]:
        total = total + ref[...]
    refs[-1][...] = total


def column_starts(m, k, count):
    per = k // LANES
    return [
        (r // (m * per)) * m * k + (r % m) * k + (r // m % per) * LANES for r in range(count)
    ]


def score(total, m, k, target_high, target_low, squares, out):
    exs = total.shape[0]
    starts = column_starts(m, k, total.shape[1])
    order = sorted(range(len(starts)), key=lambda r: starts[r])
    rows = jnp.concatenate([total[:, r, :] for r in order], axis=1)
    pair = jnp.concatenate(halves(rows), axis=0)
    both = contract_last(pair, target_high[...]) + contract_last(pair, target_low[...])
    count = target_high.shape[0]
    out[...] = jnp.zeros_like(out)
    out[0:exs, 0:count] = both[:exs] + both[exs:]
    out[0:exs, count : 2 * count] = jnp.broadcast_to(squares[...], (exs, count))
    out[exs : 2 * exs, :] = jnp.broadcast_to(
        jnp.sum(rows * rows, axis=1, keepdims=True), (exs, out.shape[1])
    )


def gathered_kernel(exs, cols, m, k, received, target_high, target_low, squares, own, out):
    def collect(x):
        total = x[:, 0]
        for i in range(1, cols):
            total = total + x[:, i]
        return total

    x = received[...]
    score(
        collect(x.reshape((exs, cols) + x.shape[1:])), m, k, target_high, target_low, squares, out
    )
    mine = received[pl.ds(lax.axis_index("ex") * cols, cols)]
    own[...] = collect(mine[None])[0]


def paired_kernel(m, k, own, other, *refs):
    *tables, local, remote = refs
    blocks = jnp.concatenate([own[...][None], other[...][None]], axis=0)
    starts = column_starts(m, k, blocks.shape[1])
    order = sorted(range(len(starts)), key=lambda r: starts[r])
    rows = jnp.concatenate([blocks[:, r, :] for r in order], axis=1)
    pair = jnp.concatenate(halves(rows), axis=0)
    lines = []
    for at in range(0, len(tables), 3):
        high, low, squares = tables[at : at + 3]
        both = contract_last(pair, high[...]) + contract_last(pair, low[...])
        scores = both[:2] + both[2:]
        lines.append(
            jnp.concatenate([scores, jnp.broadcast_to(squares[...], scores.shape)], axis=1)
        )
    square = jnp.broadcast_to(jnp.sum(rows[:1] * rows[:1], axis=1, keepdims=True), lines[0][:1].shape)
    pad = jnp.zeros((8 - len(lines), square.shape[1]), f32)
    local[...] = jnp.concatenate([line[:1] for line in lines] + [square, pad[1:]], axis=0)
    remote[...] = jnp.concatenate([line[1:] for line in lines] + [pad], axis=0)


def send_kernel(local, remote, *refs):
    *outs, table = refs
    table[0:2] = local[0:2]
    table[2:4] = remote[0:2]
    mine = lax.axis_index("ex") ^ lax.axis_index("col")
    for step, out in enumerate(outs):
        out[...] = jnp.concatenate(
            [table[pl.ds(mine ^ step, 1), :], local[2:8], local[7:8]], axis=0
        )


def last_kernel(all_cols, m, k, own, *refs):
    parts, (features, scores) = refs[:-2], refs[-2:]
    total = parts[0][...]
    for part in parts[1:]:
        total = total + part[...]
    count = scores.shape[1]
    scale = lax.rsqrt(total[1:2, 0:1] / all_cols + epsilon)
    target_scale = lax.rsqrt(total[0:1, count : 2 * count] / all_cols + epsilon)
    scores[...] = total[0:1, 0:count] * scale * target_scale / math.sqrt(all_cols)
    block = own[...] * scale
    for r, at in enumerate(column_starts(m, k, block.shape[0])):
        features[:, at : at + LANES] = block[r : r + 1]


def call(kernel, out_shape, in_specs, name, limit, scratch=(), flops=0, moved=0):
    single = not isinstance(out_shape, list)
    return pl.pallas_call(
        kernel,
        out_shape=out_shape,
        in_specs=in_specs,
        out_specs=VMEM if single else [VMEM] * len(out_shape),
        scratch_shapes=scratch,
        compiler_params=pltpu.CompilerParams(vmem_limit_bytes=limit * MIB),
        cost_estimate=pl.CostEstimate(flops=flops, bytes_accessed=moved, transcendentals=0),
        name=name,
    )


def on_device(
    hidden_input,
    output_gradient,
    lengths,
    adapter_down,
    adapter_up,
    left_sign_words,
    right_sign_words,
    targets,
    *,
    exs,
    cols,
):
    _, layers, seq, width = hidden_input.shape
    m = right_sign_words.shape[3]
    rank = adapter_down.shape[1]
    k = left_sign_words.shape[2] * WORD
    count, own_cols = targets.shape
    all_cols = own_cols * cols
    right = jnp.swapaxes(right_sign_words, 2, 3)
    neighbours = shift(targets, "ex", exs, 1)
    rows = jax.ShapeDtypeStruct(hidden_input.shape, bf16)
    mixed, hidden, grad = call(
        mix_kernel,
        [jax.ShapeDtypeStruct((layers * 2 * m, seq), f32), rows, rows],
        [HBM] * 5,
        "mix",
        8,
        [
            pltpu.VMEM(right.shape, jnp.int32),
            pltpu.VMEM((layers, rank, width), bf16),
            pltpu.VMEM((layers, width, rank), bf16),
            pltpu.SemaphoreType.DMA((4 * layers + 1,)),
        ],
        4 * layers * seq * width * rank,
        4 * MIB,
    )(*in_hbm(right, hidden_input, output_gradient, adapter_down, adapter_up))
    others = [shift(mixed, "col", cols, s) for s in range(cols - 1, 0, -1)]
    signed = jax.ShapeDtypeStruct((layers, 2, k, seq), bf16)
    high, low = call(
        sign_kernel,
        [signed, signed],
        [VMEM] * 3,
        "sign",
        8,
        [pltpu.VMEM((2, k, width), bf16)],
        4 * layers * k * seq * width,
        6 * MIB,
    )(left_sign_words, hidden, grad)
    target_half = jax.ShapeDtypeStruct(targets.shape, bf16)
    split = call(
        split_kernel,
        [target_half, target_half, jax.ShapeDtypeStruct((1, count), f32)],
        [VMEM],
        "split",
        4,
        moved=MIB,
    )
    block = (own_cols // LANES, LANES)
    lanes = -(-2 * count // LANES) * LANES
    shape = jax.ShapeDtypeStruct(block, f32)
    packed = jax.ShapeDtypeStruct((2 * exs, lanes), f32)
    results = [
        jax.ShapeDtypeStruct((1, own_cols), f32),
        jax.ShapeDtypeStruct((1, count * exs // cols), f32),
    ]
    inputs = (lengths.reshape(1, 1), mixed, *others, high, low)
    last = functools.partial(last_kernel, all_cols, m, k)
    if exs == 4 and cols == 4:
        blocks = call(
            functools.partial(pair_kernel, cols),
            [shape] * cols,
            [VMEM] * len(inputs),
            "sketch",
            8,
            [pltpu.VMEM((cols,) + block, f32)],
        )(*inputs)
        received = [shift(blocks[s], "col", cols, s) for s in STEPS]
        own = call(sum_kernel, shape, [VMEM] * cols, "own", 2)(blocks[0], *received)
        other = shift(own, "ex", exs, 2)
        line = jax.ShapeDtypeStruct((8, lanes), f32)
        local, remote = call(
            functools.partial(paired_kernel, m, k), [line, line], [VMEM] * 8, "score", 8
        )(own, other, *split(targets), *split(neighbours))
        lines = call(
            send_kernel, [line] * cols, [VMEM] * 2, "send", 2, [pltpu.VMEM((4, lanes), f32)]
        )(local, shift(remote, "ex", exs, 2))
        parts = [lines[0]] + [shift(lines[s], "col", cols, s) for s in STEPS]
        return tuple(
            call(last, results, [VMEM] * (1 + len(parts)), "last", 2)(own, *parts)
        )
    blocks = call(
        functools.partial(spread_kernel, exs, cols),
        jax.ShapeDtypeStruct((exs * cols,) + block, f32),
        [VMEM] * len(inputs),
        "sketch",
        8,
    )(*inputs)
    received = lax.all_to_all(blocks, ("ex", "col"), 0, 0, tiled=True)
    own, packed = call(
        functools.partial(gathered_kernel, exs, cols, m, k), [shape, packed], [VMEM] * 4, "score", 16
    )(received, *split(targets))
    per = exs // cols
    rows = jnp.stack([packed[:exs], packed[exs:]], axis=1)
    grid = jnp.zeros((exs, cols) + rows.shape[1:], f32)
    grid = grid.at[:, lax.axis_index("ex") // per].set(rows)
    back = lax.all_to_all(
        grid.reshape((exs * cols,) + rows.shape[1:]), ("ex", "col"), 0, 0, tiled=True
    ).reshape((exs, cols) + rows.shape[1:])
    mine = lax.dynamic_slice_in_dim(back, lax.axis_index("col") * per, per, axis=0).sum(axis=1)
    total = jnp.concatenate(
        [
            jnp.concatenate([mine[:, 0, :count].reshape(1, -1), mine[:, 0, count : 2 * count].reshape(1, -1)], axis=1),
            jnp.broadcast_to(mine[:1, 1, :1], (1, 2 * count * per)),
        ],
        axis=0,
    )
    return tuple(
        call(last, results, [VMEM] * 2, "last", 2)(own, total)
    )


def solution(mesh):
    body = functools.partial(on_device, exs=mesh.shape["ex"], cols=mesh.shape["col"])
    return jax.shard_map(
        body,
        mesh=mesh,
        in_specs=(
            P(("grp", "ex"), None, None, "col"),
            P(("grp", "ex"), None, None, "col"),
            P(("grp", "ex")),
            P(None, None, "col"),
            P(None, "col", None),
            P(None, None, None, "col"),
            P(),
            P(("grp", "ex"), "col"),
        ),
        out_specs=(P(("grp", "ex"), "col"), P(("grp", "ex"), "col")),
        check_vma=False,
    )
```

```python
import functools
import math

import jax
import jax.numpy as jnp
from jax import lax
from jax.experimental import pallas as pl
from jax.experimental.pallas import tpu as pltpu
from jax.sharding import PartitionSpec as P

epsilon = 1e-06
WORD = 16
STEPS = (1, 2, 3)
LANES = 128
f32, bf16 = jnp.float32, jnp.bfloat16
MIB = 1 << 20

VMEM = pl.BlockSpec(memory_space=pltpu.VMEM)
HBM = pl.BlockSpec(memory_space=pltpu.HBM)


def contract_last(a, b):
    return lax.dot_general(a, b, (((1,), (1,)), ((), ())), preferred_element_type=f32)


def product(a, b):
    return jnp.dot(a, b, preferred_element_type=f32)


def halves(x):
    high = x.astype(bf16)
    return high, (x - high.astype(f32)).astype(bf16)


def partner(i, step, count):
    return i ^ step if count & (count - 1) == 0 else (i + step) % count


def shift(x, axis, count, step):
    return lax.ppermute(x, axis, [(i, partner(i, step, count)) for i in range(count)])


def in_hbm(*arrays):
    return [pltpu.with_memory_space_constraint(x, pltpu.HBM) for x in arrays]


def mix_kernel(
    right, hidden, grad, down, up, out, hid_out, grad_out, right_buf, down_buf, up_buf, sems
):
    layers = hidden.shape[1]
    sides = [(l, j) for l in range(layers) for j in range(2)]
    first = [(right, right_buf)]
    first += [((up if j else down).at[l], (up_buf if j else down_buf).at[l]) for l, j in sides]
    rows = [
        ((grad if j else hidden).at[0, l], (grad_out if j else hid_out).at[0, l]) for l, j in sides
    ]
    copies = [pltpu.make_async_copy(a, b, sems.at[i]) for i, (a, b) in enumerate(first + rows)]
    for copy in copies:
        copy.start()
    for copy in copies[: len(first)]:
        copy.wait()
    pairs = []
    for l, j in sides:
        signs = (2 * right_buf[l, j] - 1).astype(f32).astype(bf16)
        if j == 0:
            folded = product(signs, down_buf[l])
        else:
            folded = contract_last(signs, up_buf[l])
        pairs.append(jnp.concatenate(halves(folded), axis=0))
    for copy in copies[len(first) :]:
        copy.wait()
    for at, (l, j) in enumerate(sides):
        both = contract_last(pairs[at], (grad_out if j else hid_out)[0, l])
        m = both.shape[0] // 2
        out[at * m : (at + 1) * m, :] = both[:m] + both[m:]


def unpack(words, l, j, out):
    bits = 1 << lax.broadcasted_iota(jnp.int32, (WORD, 1), 0)
    width = words.shape[3]
    for w in range(words.shape[2]):
        word = jnp.broadcast_to(words[l, j, w : w + 1, :], (WORD, width))
        signs = jnp.where((word & bits) != 0, 1.0, -1.0)
        out[w * WORD : (w + 1) * WORD, :] = signs.astype(f32).astype(bf16)


def split_kernel(targets, high, low, squares):
    t = targets[...]
    high[...], low[...] = halves(t)
    squares[...] = jnp.transpose(jnp.sum(t * t, axis=1, keepdims=True))


def sign_kernel(words, hidden, grad, high, low, signs):
    items = [(l, j) for l in range(hidden.shape[1]) for j in range(2)]
    unpack(words, *items[0], signs.at[0])
    for i, (l, j) in enumerate(items):
        if i + 1 < len(items):
            unpack(words, *items[i + 1], signs.at[(i + 1) % 2])
        signed = contract_last((grad if j == 0 else hidden)[0, l], signs[i % 2])
        high[l, j], low[l, j] = halves(signed)


def sketch_blocks(cols, length, own, others, high, low):
    mixed = own[...]
    for other in others:
        mixed = mixed + other[...]
    n = length[...]
    positions = lax.broadcasted_iota(jnp.int32, (1, mixed.shape[1]), 1)
    mixed = mixed * jnp.where(positions < n, 1.0 / n.astype(f32), 0.0)
    layers, sides, _, k = high.shape
    m = mixed.shape[0] // (layers * sides)
    pieces = []
    for l in range(layers):
        for j in range(sides):
            base = (2 * l + j) * m
            pair = jnp.concatenate(halves(mixed[base : base + m]), axis=0)
            both = product(pair, high[l, j]) + product(pair, low[l, j])
            both = both[:m] + both[m:]
            pieces += [both[:, q : q + LANES] for q in range(0, k, LANES)]
    per = len(pieces) // cols
    return [jnp.concatenate(pieces[i * per : (i + 1) * per], axis=0) for i in range(cols)]


def spread_kernel(exs, cols, length, own, *refs):
    others, (high, low, out) = refs[: cols - 1], refs[cols - 1 :]
    for i, block in enumerate(sketch_blocks(cols, length, own, others, high, low)):
        for e in range(exs):
            out[e * cols + i] = block


def pair_kernel(cols, length, own, *refs):
    others, (high, low), outs, table = refs[: cols - 1], refs[cols - 1 : cols + 1], refs[cols + 1 : -1], refs[-1]
    for i, block in enumerate(sketch_blocks(cols, length, own, others, high, low)):
        table[i] = block
    me = lax.axis_index("col")
    for step, out in enumerate(outs):
        out[...] = table[partner(me, step, cols)]


def sum_kernel(*refs):
    total = refs[0][...]
    for ref in refs[1:-1]:
        total = total + ref[...]
    refs[-1][...] = total


def column_starts(m, k, count):
    per = k // LANES
    return [
        (r // (m * per)) * m * k + (r % m) * k + (r // m % per) * LANES for r in range(count)
    ]


def score(total, m, k, target_high, target_low, squares, out):
    exs = total.shape[0]
    starts = column_starts(m, k, total.shape[1])
    order = sorted(range(len(starts)), key=lambda r: starts[r])
    rows = jnp.concatenate([total[:, r, :] for r in order], axis=1)
    pair = jnp.concatenate(halves(rows), axis=0)
    both = contract_last(pair, target_high[...]) + contract_last(pair, target_low[...])
    count = target_high.shape[0]
    out[...] = jnp.zeros_like(out)
    out[0:exs, 0:count] = both[:exs] + both[exs:]
    out[0:exs, count : 2 * count] = jnp.broadcast_to(squares[...], (exs, count))
    out[exs : 2 * exs, :] = jnp.broadcast_to(
        jnp.sum(rows * rows, axis=1, keepdims=True), (exs, out.shape[1])
    )


def gathered_kernel(exs, cols, m, k, received, target_high, target_low, squares, own, out):
    def collect(x):
        total = x[:, 0]
        for i in range(1, cols):
            total = total + x[:, i]
        return total

    x = received[...]
    score(
        collect(x.reshape((exs, cols) + x.shape[1:])), m, k, target_high, target_low, squares, out
    )
    mine = received[pl.ds(lax.axis_index("ex") * cols, cols)]
    own[...] = collect(mine[None])[0]


def paired_kernel(m, k, own, other, *refs):
    *tables, local, remote = refs
    blocks = jnp.concatenate([own[...][None], other[...][None]], axis=0)
    starts = column_starts(m, k, blocks.shape[1])
    order = sorted(range(len(starts)), key=lambda r: starts[r])
    rows = jnp.concatenate([blocks[:, r, :] for r in order], axis=1)
    pair = jnp.concatenate(halves(rows), axis=0)
    lines = []
    for at in range(0, len(tables), 3):
        high, low, squares = tables[at : at + 3]
        both = contract_last(pair, high[...]) + contract_last(pair, low[...])
        scores = both[:2] + both[2:]
        lines.append(
            jnp.concatenate([scores, jnp.broadcast_to(squares[...], scores.shape)], axis=1)
        )
    square = jnp.broadcast_to(jnp.sum(rows[:1] * rows[:1], axis=1, keepdims=True), lines[0][:1].shape)
    pad = jnp.zeros((8 - len(lines), square.shape[1]), f32)
    local[...] = jnp.concatenate([line[:1] for line in lines] + [square, pad[1:]], axis=0)
    remote[...] = jnp.concatenate([line[1:] for line in lines] + [pad], axis=0)


def send_kernel(local, remote, *refs):
    *outs, table = refs
    table[0:2] = local[0:2]
    table[2:4] = remote[0:2]
    mine = lax.axis_index("ex") ^ lax.axis_index("col")
    for step, out in enumerate(outs):
        out[...] = jnp.concatenate(
            [table[pl.ds(mine ^ step, 1), :], local[2:8], local[7:8]], axis=0
        )


def last_kernel(all_cols, m, k, own, *refs):
    parts, (features, scores) = refs[:-2], refs[-2:]
    total = parts[0][...]
    for part in parts[1:]:
        total = total + part[...]
    count = scores.shape[1]
    scale = lax.rsqrt(total[1:2, 0:1] / all_cols + epsilon)
    target_scale = lax.rsqrt(total[0:1, count : 2 * count] / all_cols + epsilon)
    scores[...] = total[0:1, 0:count] * scale * target_scale / math.sqrt(all_cols)
    block = own[...] * scale
    for r, at in enumerate(column_starts(m, k, block.shape[0])):
        features[:, at : at + LANES] = block[r : r + 1]


def call(kernel, out_shape, in_specs, name, limit, scratch=(), flops=0, moved=0):
    single = not isinstance(out_shape, list)
    return pl.pallas_call(
        kernel,
        out_shape=out_shape,
        in_specs=in_specs,
        out_specs=VMEM if single else [VMEM] * len(out_shape),
        scratch_shapes=scratch,
        compiler_params=pltpu.CompilerParams(vmem_limit_bytes=limit * MIB),
        cost_estimate=pl.CostEstimate(flops=flops, bytes_accessed=moved, transcendentals=0),
        name=name,
    )


def on_device(
    hidden_input,
    output_gradient,
    lengths,
    adapter_down,
    adapter_up,
    left_sign_words,
    right_sign_words,
    targets,
    *,
    exs,
    cols,
):
    _, layers, seq, width = hidden_input.shape
    m = right_sign_words.shape[3]
    rank = adapter_down.shape[1]
    k = left_sign_words.shape[2] * WORD
    count, own_cols = targets.shape
    all_cols = own_cols * cols
    right = jnp.swapaxes(right_sign_words, 2, 3)
    neighbours = shift(targets, "ex", exs, 1)
    rows = jax.ShapeDtypeStruct(hidden_input.shape, bf16)
    mixed, hidden, grad = call(
        mix_kernel,
        [jax.ShapeDtypeStruct((layers * 2 * m, seq), f32), rows, rows],
        [HBM] * 5,
        "mix",
        8,
        [
            pltpu.VMEM(right.shape, jnp.int32),
            pltpu.VMEM((layers, rank, width), bf16),
            pltpu.VMEM((layers, width, rank), bf16),
            pltpu.SemaphoreType.DMA((4 * layers + 1,)),
        ],
        4 * layers * seq * width * rank,
        4 * MIB,
    )(*in_hbm(right, hidden_input, output_gradient, adapter_down, adapter_up))
    others = [shift(mixed, "col", cols, s) for s in range(cols - 1, 0, -1)]
    signed = jax.ShapeDtypeStruct((layers, 2, seq, k), bf16)
    high, low = call(
        sign_kernel,
        [signed, signed],
        [VMEM] * 3,
        "sign",
        8,
        [pltpu.VMEM((2, k, width), bf16)],
        4 * layers * k * seq * width,
        6 * MIB,
    )(left_sign_words, hidden, grad)
    target_half = jax.ShapeDtypeStruct(targets.shape, bf16)
    split = call(
        split_kernel,
        [target_half, target_half, jax.ShapeDtypeStruct((1, count), f32)],
        [VMEM],
        "split",
        4,
        moved=MIB,
    )
    block = (own_cols // LANES, LANES)
    lanes = -(-2 * count // LANES) * LANES
    shape = jax.ShapeDtypeStruct(block, f32)
    packed = jax.ShapeDtypeStruct((2 * exs, lanes), f32)
    results = [
        jax.ShapeDtypeStruct((1, own_cols), f32),
        jax.ShapeDtypeStruct((1, count * exs // cols), f32),
    ]
    inputs = (lengths.reshape(1, 1), mixed, *others, high, low)
    last = functools.partial(last_kernel, all_cols, m, k)
    if exs == 4 and cols == 4:
        blocks = call(
            functools.partial(pair_kernel, cols),
            [shape] * cols,
            [VMEM] * len(inputs),
            "sketch",
            8,
            [pltpu.VMEM((cols,) + block, f32)],
        )(*inputs)
        received = [shift(blocks[s], "col", cols, s) for s in STEPS]
        own = call(sum_kernel, shape, [VMEM] * cols, "own", 2)(blocks[0], *received)
        other = shift(own, "ex", exs, 2)
        line = jax.ShapeDtypeStruct((8, lanes), f32)
        local, remote = call(
            functools.partial(paired_kernel, m, k), [line, line], [VMEM] * 8, "score", 8
        )(own, other, *split(targets), *split(neighbours))
        lines = call(
            send_kernel, [line] * cols, [VMEM] * 2, "send", 2, [pltpu.VMEM((4, lanes), f32)]
        )(local, shift(remote, "ex", exs, 2))
        parts = [lines[0]] + [shift(lines[s], "col", cols, s) for s in STEPS]
        return tuple(
            call(last, results, [VMEM] * (1 + len(parts)), "last", 2)(own, *parts)
        )
    blocks = call(
        functools.partial(spread_kernel, exs, cols),
        jax.ShapeDtypeStruct((exs * cols,) + block, f32),
        [VMEM] * len(inputs),
        "sketch",
        8,
    )(*inputs)
    received = lax.all_to_all(blocks, ("ex", "col"), 0, 0, tiled=True)
    own, packed = call(
        functools.partial(gathered_kernel, exs, cols, m, k), [shape, packed], [VMEM] * 4, "score", 16
    )(received, *split(targets))
    per = exs // cols
    rows = jnp.stack([packed[:exs], packed[exs:]], axis=1)
    grid = jnp.zeros((exs, cols) + rows.shape[1:], f32)
    grid = grid.at[:, lax.axis_index("ex") // per].set(rows)
    back = lax.all_to_all(
        grid.reshape((exs * cols,) + rows.shape[1:]), ("ex", "col"), 0, 0, tiled=True
    ).reshape((exs, cols) + rows.shape[1:])
    mine = lax.dynamic_slice_in_dim(back, lax.axis_index("col") * per, per, axis=0).sum(axis=1)
    total = jnp.concatenate(
        [
            jnp.concatenate([mine[:, 0, :count].reshape(1, -1), mine[:, 0, count : 2 * count].reshape(1, -1)], axis=1),
            jnp.broadcast_to(mine[:1, 1, :1], (1, 2 * count * per)),
        ],
        axis=0,
    )
    return tuple(
        call(last, results, [VMEM] * 2, "last", 2)(own, total)
    )


def solution(mesh):
    body = functools.partial(on_device, exs=mesh.shape["ex"], cols=mesh.shape["col"])
    return jax.shard_map(
        body,
        mesh=mesh,
        in_specs=(
            P(("grp", "ex"), None, None, "col"),
            P(("grp", "ex"), None, None, "col"),
            P(("grp", "ex")),
            P(None, None, "col"),
            P(None, "col", None),
            P(None, None, None, "col"),
            P(),
            P(("grp", "ex"), "col"),
        ),
        out_specs=(P(("grp", "ex"), "col"), P(("grp", "ex"), "col")),
        check_vma=False,
    )
```

```python
import functools
import math

import jax
import jax.numpy as jnp
from jax import lax
from jax.experimental import pallas as pl
from jax.experimental.pallas import tpu as pltpu
from jax.sharding import PartitionSpec as P

epsilon = 1e-06
WORD = 16
STEPS = (1, 2, 3)
LANES = 128
f32, bf16 = jnp.float32, jnp.bfloat16
MIB = 1 << 20

def crossed(x, exs, cols):
    pairs = [(e * cols + i, (e ^ 2) * cols + (i ^ 1)) for e in range(exs) for i in range(cols)]
    return lax.ppermute(x, ("ex", "col"), pairs)


VMEM = pl.BlockSpec(memory_space=pltpu.VMEM)
HBM = pl.BlockSpec(memory_space=pltpu.HBM)


def contract_last(a, b):
    return lax.dot_general(a, b, (((1,), (1,)), ((), ())), preferred_element_type=f32)


def product(a, b):
    return jnp.dot(a, b, preferred_element_type=f32)


def halves(x):
    high = x.astype(bf16)
    return high, (x - high.astype(f32)).astype(bf16)


def partner(i, step, count):
    return i ^ step if count & (count - 1) == 0 else (i + step) % count


def shift(x, axis, count, step):
    return lax.ppermute(x, axis, [(i, partner(i, step, count)) for i in range(count)])


def in_hbm(*arrays):
    return [pltpu.with_memory_space_constraint(x, pltpu.HBM) for x in arrays]


def mix_kernel(
    right, hidden, grad, down, up, out, hid_out, grad_out, right_buf, down_buf, up_buf, sems
):
    layers = hidden.shape[1]
    sides = [(l, j) for l in range(layers) for j in range(2)]
    first = [(right, right_buf)]
    first += [((up if j else down).at[l], (up_buf if j else down_buf).at[l]) for l, j in sides]
    rows = [
        ((grad if j else hidden).at[0, l], (grad_out if j else hid_out).at[0, l]) for l, j in sides
    ]
    copies = [pltpu.make_async_copy(a, b, sems.at[i]) for i, (a, b) in enumerate(first + rows)]
    for copy in copies:
        copy.start()
    for copy in copies[: len(first)]:
        copy.wait()
    pairs = []
    for l, j in sides:
        signs = (2 * right_buf[l, j] - 1).astype(f32).astype(bf16)
        if j == 0:
            folded = product(signs, down_buf[l])
        else:
            folded = contract_last(signs, up_buf[l])
        pairs.append(jnp.concatenate(halves(folded), axis=0))
    for copy in copies[len(first) :]:
        copy.wait()
    for at, (l, j) in enumerate(sides):
        both = contract_last(pairs[at], (grad_out if j else hid_out)[0, l])
        m = both.shape[0] // 2
        out[at * m : (at + 1) * m, :] = both[:m] + both[m:]


def unpack(words, l, j, out):
    bits = 1 << lax.broadcasted_iota(jnp.int32, (WORD, 1), 0)
    width = words.shape[3]
    for w in range(words.shape[2]):
        word = jnp.broadcast_to(words[l, j, w : w + 1, :], (WORD, width))
        signs = jnp.where((word & bits) != 0, 1.0, -1.0)
        out[w * WORD : (w + 1) * WORD, :] = signs.astype(f32).astype(bf16)


def split_kernel(targets, high, low, squares):
    t = targets[...]
    high[...], low[...] = halves(t)
    squares[...] = jnp.transpose(jnp.sum(t * t, axis=1, keepdims=True))


def sign_kernel(words, hidden, grad, high, low, signs):
    items = [(l, j) for l in range(hidden.shape[1]) for j in range(2)]
    unpack(words, *items[0], signs.at[0])
    for i, (l, j) in enumerate(items):
        if i + 1 < len(items):
            unpack(words, *items[i + 1], signs.at[(i + 1) % 2])
        signed = contract_last((grad if j == 0 else hidden)[0, l], signs[i % 2])
        high[l, j], low[l, j] = halves(signed)


def sketch_blocks(cols, length, own, others, high, low):
    mixed = own[...]
    for other in others:
        mixed = mixed + other[...]
    n = length[...]
    positions = lax.broadcasted_iota(jnp.int32, (1, mixed.shape[1]), 1)
    mixed = mixed * jnp.where(positions < n, 1.0 / n.astype(f32), 0.0)
    layers, sides, _, k = high.shape
    m = mixed.shape[0] // (layers * sides)
    pieces = []
    for l in range(layers):
        for j in range(sides):
            base = (2 * l + j) * m
            pair = jnp.concatenate(halves(mixed[base : base + m]), axis=0)
            both = product(pair, high[l, j]) + product(pair, low[l, j])
            both = both[:m] + both[m:]
            pieces += [both[:, q : q + LANES] for q in range(0, k, LANES)]
    per = len(pieces) // cols
    return [jnp.concatenate(pieces[i * per : (i + 1) * per], axis=0) for i in range(cols)]


def spread_kernel(exs, cols, length, own, *refs):
    others, (high, low, out) = refs[: cols - 1], refs[cols - 1 :]
    for i, block in enumerate(sketch_blocks(cols, length, own, others, high, low)):
        for e in range(exs):
            out[e * cols + i] = block


def pair_kernel(cols, length, own, *refs):
    others, (high, low), outs, table = refs[: cols - 1], refs[cols - 1 : cols + 1], refs[cols + 1 : -1], refs[-1]
    for i, block in enumerate(sketch_blocks(cols, length, own, others, high, low)):
        table[i] = block
    me = lax.axis_index("col")
    for step, out in enumerate(outs):
        to = partner(me, step, cols)
        out[0] = table[to]
        out[1] = table[to ^ 1]


def sum_kernel(*refs):
    *parts, own, pair = refs
    total = sum(part[...] for part in parts)
    own[...] = total[0]
    pair[...] = total[1]


def column_starts(m, k, count):
    per = k // LANES
    return [
        (r // (m * per)) * m * k + (r % m) * k + (r // m % per) * LANES for r in range(count)
    ]


def score(total, m, k, target_high, target_low, squares, out):
    exs = total.shape[0]
    starts = column_starts(m, k, total.shape[1])
    order = sorted(range(len(starts)), key=lambda r: starts[r])
    rows = jnp.concatenate([total[:, r, :] for r in order], axis=1)
    pair = jnp.concatenate(halves(rows), axis=0)
    both = contract_last(pair, target_high[...]) + contract_last(pair, target_low[...])
    count = target_high.shape[0]
    out[...] = jnp.zeros_like(out)
    out[0:exs, 0:count] = both[:exs] + both[exs:]
    out[0:exs, count : 2 * count] = jnp.broadcast_to(squares[...], (exs, count))
    out[exs : 2 * exs, :] = jnp.broadcast_to(
        jnp.sum(rows * rows, axis=1, keepdims=True), (exs, out.shape[1])
    )


def gathered_kernel(exs, cols, m, k, received, target_high, target_low, squares, own, out):
    def collect(x):
        total = x[:, 0]
        for i in range(1, cols):
            total = total + x[:, i]
        return total

    x = received[...]
    score(
        collect(x.reshape((exs, cols) + x.shape[1:])), m, k, target_high, target_low, squares, out
    )
    mine = received[pl.ds(lax.axis_index("ex") * cols, cols)]
    own[...] = collect(mine[None])[0]


def paired_kernel(m, k, own, other, *refs):
    *tables, local, remote = refs
    blocks = jnp.concatenate([own[...][None], other[...][None]], axis=0)
    starts = column_starts(m, k, blocks.shape[1])
    order = sorted(range(len(starts)), key=lambda r: starts[r])
    rows = jnp.concatenate([blocks[:, r, :] for r in order], axis=1)
    pair = jnp.concatenate(halves(rows), axis=0)
    lines = []
    for at in range(0, len(tables), 3):
        high, low, squares = tables[at : at + 3]
        both = contract_last(pair, high[...]) + contract_last(pair, low[...])
        scores = both[:2] + both[2:]
        lines.append(
            jnp.concatenate([scores, jnp.broadcast_to(squares[...], scores.shape)], axis=1)
        )
    square = jnp.broadcast_to(jnp.sum(rows[:1] * rows[:1], axis=1, keepdims=True), lines[0][:1].shape)
    pad = jnp.zeros((8 - len(lines), square.shape[1]), f32)
    local[...] = jnp.concatenate([line[:1] for line in lines] + [square, pad[1:]], axis=0)
    remote[...] = jnp.concatenate([line[1:] for line in lines] + [pad], axis=0)


def send_kernel(local, remote, *refs):
    *outs, table = refs
    table[0:2] = local[0:2]
    table[2:4] = remote[0:2]
    mine = lax.axis_index("ex") ^ lax.axis_index("col")
    for step, out in enumerate(outs):
        out[...] = jnp.concatenate(
            [table[pl.ds(mine ^ step, 1), :], local[2:8], local[7:8]], axis=0
        )


def last_kernel(all_cols, m, k, own, *refs):
    parts, (features, scores) = refs[:-2], refs[-2:]
    total = parts[0][...]
    for part in parts[1:]:
        total = total + part[...]
    count = scores.shape[1]
    scale = lax.rsqrt(total[1:2, 0:1] / all_cols + epsilon)
    target_scale = lax.rsqrt(total[0:1, count : 2 * count] / all_cols + epsilon)
    scores[...] = total[0:1, 0:count] * scale * target_scale / math.sqrt(all_cols)
    block = own[...] * scale
    for r, at in enumerate(column_starts(m, k, block.shape[0])):
        features[:, at : at + LANES] = block[r : r + 1]


def call(kernel, out_shape, in_specs, name, limit, scratch=(), flops=0, moved=0):
    single = not isinstance(out_shape, list)
    return pl.pallas_call(
        kernel,
        out_shape=out_shape,
        in_specs=in_specs,
        out_specs=VMEM if single else [VMEM] * len(out_shape),
        scratch_shapes=scratch,
        compiler_params=pltpu.CompilerParams(vmem_limit_bytes=limit * MIB),
        cost_estimate=pl.CostEstimate(flops=flops, bytes_accessed=moved, transcendentals=0),
        name=name,
    )


def on_device(
    hidden_input,
    output_gradient,
    lengths,
    adapter_down,
    adapter_up,
    left_sign_words,
    right_sign_words,
    targets,
    *,
    exs,
    cols,
):
    _, layers, seq, width = hidden_input.shape
    m = right_sign_words.shape[3]
    rank = adapter_down.shape[1]
    k = left_sign_words.shape[2] * WORD
    count, own_cols = targets.shape
    all_cols = own_cols * cols
    right = jnp.swapaxes(right_sign_words, 2, 3)
    neighbours = shift(targets, "ex", exs, 1)
    rows = jax.ShapeDtypeStruct(hidden_input.shape, bf16)
    mixed, hidden, grad = call(
        mix_kernel,
        [jax.ShapeDtypeStruct((layers * 2 * m, seq), f32), rows, rows],
        [HBM] * 5,
        "mix",
        8,
        [
            pltpu.VMEM(right.shape, jnp.int32),
            pltpu.VMEM((layers, rank, width), bf16),
            pltpu.VMEM((layers, width, rank), bf16),
            pltpu.SemaphoreType.DMA((4 * layers + 1,)),
        ],
        4 * layers * seq * width * rank,
        4 * MIB,
    )(*in_hbm(right, hidden_input, output_gradient, adapter_down, adapter_up))
    others = [shift(mixed, "col", cols, s) for s in range(cols - 1, 0, -1)]
    signed = jax.ShapeDtypeStruct((layers, 2, seq, k), bf16)
    high, low = call(
        sign_kernel,
        [signed, signed],
        [VMEM] * 3,
        "sign",
        8,
        [pltpu.VMEM((2, k, width), bf16)],
        4 * layers * k * seq * width,
        6 * MIB,
    )(left_sign_words, hidden, grad)
    target_half = jax.ShapeDtypeStruct(targets.shape, bf16)
    split = call(
        split_kernel,
        [target_half, target_half, jax.ShapeDtypeStruct((1, count), f32)],
        [VMEM],
        "split",
        4,
        moved=MIB,
    )
    block = (own_cols // LANES, LANES)
    lanes = -(-2 * count // LANES) * LANES
    shape = jax.ShapeDtypeStruct(block, f32)
    packed = jax.ShapeDtypeStruct((2 * exs, lanes), f32)
    results = [
        jax.ShapeDtypeStruct((1, own_cols), f32),
        jax.ShapeDtypeStruct((1, count * exs // cols), f32),
    ]
    inputs = (lengths.reshape(1, 1), mixed, *others, high, low)
    last = functools.partial(last_kernel, all_cols, m, k)
    if exs == 4 and cols == 4:
        blocks = call(
            functools.partial(pair_kernel, cols),
            [jax.ShapeDtypeStruct((2,) + block, f32)] * cols,
            [VMEM] * len(inputs),
            "sketch",
            8,
            [pltpu.VMEM((cols,) + block, f32)],
        )(*inputs)
        received = [shift(blocks[s], "col", cols, s) for s in STEPS]
        own, pair = call(sum_kernel, [shape] * 2, [VMEM] * cols, "own", 2)(blocks[0], *received)
        other = crossed(pair, exs, cols)
        line = jax.ShapeDtypeStruct((8, lanes), f32)
        local, remote = call(
            functools.partial(paired_kernel, m, k), [line, line], [VMEM] * 8, "score", 8
        )(own, other, *split(targets), *split(neighbours))
        lines = call(
            send_kernel, [line] * cols, [VMEM] * 2, "send", 2, [pltpu.VMEM((4, lanes), f32)]
        )(local, crossed(remote, exs, cols))
        parts = [lines[0]] + [shift(lines[s], "col", cols, s) for s in STEPS]
        return tuple(
            call(last, results, [VMEM] * (1 + len(parts)), "last", 2)(own, *parts)
        )
    blocks = call(
        functools.partial(spread_kernel, exs, cols),
        jax.ShapeDtypeStruct((exs * cols,) + block, f32),
        [VMEM] * len(inputs),
        "sketch",
        8,
    )(*inputs)
    received = lax.all_to_all(blocks, ("ex", "col"), 0, 0, tiled=True)
    own, packed = call(
        functools.partial(gathered_kernel, exs, cols, m, k), [shape, packed], [VMEM] * 4, "score", 16
    )(received, *split(targets))
    per = exs // cols
    rows = jnp.stack([packed[:exs], packed[exs:]], axis=1)
    grid = jnp.zeros((exs, cols) + rows.shape[1:], f32)
    grid = grid.at[:, lax.axis_index("ex") // per].set(rows)
    back = lax.all_to_all(
        grid.reshape((exs * cols,) + rows.shape[1:]), ("ex", "col"), 0, 0, tiled=True
    ).reshape((exs, cols) + rows.shape[1:])
    mine = lax.dynamic_slice_in_dim(back, lax.axis_index("col") * per, per, axis=0).sum(axis=1)
    total = jnp.concatenate(
        [
            jnp.concatenate([mine[:, 0, :count].reshape(1, -1), mine[:, 0, count : 2 * count].reshape(1, -1)], axis=1),
            jnp.broadcast_to(mine[:1, 1, :1], (1, 2 * count * per)),
        ],
        axis=0,
    )
    return tuple(
        call(last, results, [VMEM] * 2, "last", 2)(own, total)
    )


def solution(mesh):
    body = functools.partial(on_device, exs=mesh.shape["ex"], cols=mesh.shape["col"])
    return jax.shard_map(
        body,
        mesh=mesh,
        in_specs=(
            P(("grp", "ex"), None, None, "col"),
            P(("grp", "ex"), None, None, "col"),
            P(("grp", "ex")),
            P(None, None, "col"),
            P(None, "col", None),
            P(None, None, None, "col"),
            P(),
            P(("grp", "ex"), "col"),
        ),
        out_specs=(P(("grp", "ex"), "col"), P(("grp", "ex"), "col")),
        check_vma=False,
    )
```

```python
import functools
import math

import jax
import jax.numpy as jnp
from jax import lax
from jax.experimental import pallas as pl
from jax.experimental.pallas import tpu as pltpu
from jax.sharding import PartitionSpec as P

epsilon = 1e-06
WORD = 16
STEPS = (1, 2, 3)
LANES = 128
f32, bf16 = jnp.float32, jnp.bfloat16
MIB = 1 << 20

def crossed(x, exs, cols):
    pairs = [(e * cols + i, (e ^ 2) * cols + (i ^ 1)) for e in range(exs) for i in range(cols)]
    return lax.ppermute(x, ("ex", "col"), pairs)


VMEM = pl.BlockSpec(memory_space=pltpu.VMEM)
HBM = pl.BlockSpec(memory_space=pltpu.HBM)


def contract_last(a, b):
    return lax.dot_general(a, b, (((1,), (1,)), ((), ())), preferred_element_type=f32)


def product(a, b):
    return jnp.dot(a, b, preferred_element_type=f32)


def halves(x):
    high = x.astype(bf16)
    return high, (x - high.astype(f32)).astype(bf16)


def partner(i, step, count):
    return i ^ step if count & (count - 1) == 0 else (i + step) % count


def shift(x, axis, count, step):
    return lax.ppermute(x, axis, [(i, partner(i, step, count)) for i in range(count)])


def in_hbm(*arrays):
    return [pltpu.with_memory_space_constraint(x, pltpu.HBM) for x in arrays]


def mix_kernel(
    right, hidden, grad, down, up, out, hid_out, grad_out, right_buf, down_buf, up_buf, sems
):
    layers = hidden.shape[1]
    sides = [(l, j) for l in range(layers) for j in range(2)]
    first = [(right, right_buf)]
    first += [((up if j else down).at[l], (up_buf if j else down_buf).at[l]) for l, j in sides]
    rows = [
        ((grad if j else hidden).at[0, l], (grad_out if j else hid_out).at[0, l]) for l, j in sides
    ]
    copies = [pltpu.make_async_copy(a, b, sems.at[i]) for i, (a, b) in enumerate(first + rows)]
    for copy in copies:
        copy.start()
    for copy in copies[: len(first)]:
        copy.wait()
    pairs = []
    for l, j in sides:
        signs = (2 * right_buf[l, j] - 1).astype(f32).astype(bf16)
        if j == 0:
            folded = product(signs, down_buf[l])
        else:
            folded = contract_last(signs, up_buf[l])
        pairs.append(jnp.concatenate(halves(folded), axis=0))
    for copy in copies[len(first) :]:
        copy.wait()
    for at, (l, j) in enumerate(sides):
        both = contract_last(pairs[at], (grad_out if j else hid_out)[0, l])
        m = both.shape[0] // 2
        out[at * m : (at + 1) * m, :] = both[:m] + both[m:]


def unpack(words, l, j, out):
    bits = 1 << lax.broadcasted_iota(jnp.int32, (WORD, 1), 0)
    width = words.shape[3]
    for w in range(words.shape[2]):
        word = jnp.broadcast_to(words[l, j, w : w + 1, :], (WORD, width))
        signs = jnp.where((word & bits) != 0, 1.0, -1.0)
        out[w * WORD : (w + 1) * WORD, :] = signs.astype(f32).astype(bf16)


def split_kernel(*refs):
    *targets, table, squares = refs
    t = jnp.concatenate([ref[...] for ref in targets], axis=0)
    turned = jnp.transpose(t)
    count = turned.shape[1]
    table[:, :count], table[:, count:] = halves(turned)
    squares[...] = jnp.sum(turned * turned, axis=0, keepdims=True)


def sign_kernel(words, hidden, grad, high, low, signs):
    items = [(l, j) for l in range(hidden.shape[1]) for j in range(2)]
    unpack(words, *items[0], signs.at[0])
    for i, (l, j) in enumerate(items):
        if i + 1 < len(items):
            unpack(words, *items[i + 1], signs.at[(i + 1) % 2])
        signed = contract_last((grad if j == 0 else hidden)[0, l], signs[i % 2])
        high[l, j], low[l, j] = halves(signed)


def sketch_blocks(cols, length, own, others, high, low):
    mixed = own[...]
    for other in others:
        mixed = mixed + other[...]
    n = length[...]
    positions = lax.broadcasted_iota(jnp.int32, (1, mixed.shape[1]), 1)
    mixed = mixed * jnp.where(positions < n, 1.0 / n.astype(f32), 0.0)
    layers, sides, _, k = high.shape
    m = mixed.shape[0] // (layers * sides)
    pieces = []
    for l in range(layers):
        for j in range(sides):
            base = (2 * l + j) * m
            pair = jnp.concatenate(halves(mixed[base : base + m]), axis=0)
            both = product(pair, high[l, j]) + product(pair, low[l, j])
            both = both[:m] + both[m:]
            pieces += [both[:, q : q + LANES] for q in range(0, k, LANES)]
    per = len(pieces) // cols
    return [jnp.concatenate(pieces[i * per : (i + 1) * per], axis=0) for i in range(cols)]


def spread_kernel(exs, cols, length, own, *refs):
    others, (high, low, out) = refs[: cols - 1], refs[cols - 1 :]
    for i, block in enumerate(sketch_blocks(cols, length, own, others, high, low)):
        for e in range(exs):
            out[e * cols + i] = block


def pair_kernel(cols, length, own, *refs):
    others, (high, low), outs, table = refs[: cols - 1], refs[cols - 1 : cols + 1], refs[cols + 1 : -1], refs[-1]
    for i, block in enumerate(sketch_blocks(cols, length, own, others, high, low)):
        table[i] = block
    me = lax.axis_index("col")
    for step, out in enumerate(outs):
        to = partner(me, step, cols)
        out[0] = table[to]
        out[1] = table[to ^ 1]


def sum_kernel(*refs):
    *parts, own, pair = refs
    total = sum(part[...] for part in parts)
    own[...] = total[0]
    pair[...] = total[1]


def column_starts(m, k, count):
    per = k // LANES
    return [
        (r // (m * per)) * m * k + (r % m) * k + (r // m % per) * LANES for r in range(count)
    ]


def score(total, m, k, table, squares, out):
    exs = total.shape[0]
    starts = column_starts(m, k, total.shape[1])
    order = sorted(range(len(starts)), key=lambda r: starts[r])
    rows = jnp.concatenate([total[:, r, :] for r in order], axis=1)
    pair = jnp.concatenate(halves(rows), axis=0)
    both = product(pair, table[...])
    count = squares.shape[1]
    both = both[:, :count] + both[:, count:]
    out[...] = jnp.zeros_like(out)
    out[0:exs, 0:count] = both[:exs] + both[exs:]
    out[0:exs, count : 2 * count] = jnp.broadcast_to(squares[...], (exs, count))
    out[exs : 2 * exs, :] = jnp.broadcast_to(
        jnp.sum(rows * rows, axis=1, keepdims=True), (exs, out.shape[1])
    )


def gathered_kernel(exs, cols, m, k, received, table, squares, own, out):
    def collect(x):
        total = x[:, 0]
        for i in range(1, cols):
            total = total + x[:, i]
        return total

    x = received[...]
    score(
        collect(x.reshape((exs, cols) + x.shape[1:])), m, k, table, squares, out
    )
    mine = received[pl.ds(lax.axis_index("ex") * cols, cols)]
    own[...] = collect(mine[None])[0]


def paired_kernel(m, k, own, other, table, squares, local, remote):
    blocks = jnp.concatenate([own[...][None], other[...][None]], axis=0)
    starts = column_starts(m, k, blocks.shape[1])
    order = sorted(range(len(starts)), key=lambda r: starts[r])
    rows = jnp.concatenate([blocks[:, r, :] for r in order], axis=1)
    pair = jnp.concatenate(halves(rows), axis=0)
    both = product(pair, table[...])
    both = both[:2] + both[2:]
    total = squares.shape[1]
    both = both[:, :total] + both[:, total:]
    count = total // 2
    q = squares[...]
    for out, row in ((local, 0), (remote, 1)):
        out[...] = jnp.zeros_like(out)
        for u in range(2):
            at = slice(u * count, (u + 1) * count)
            out[u : u + 1, 0:count] = both[row : row + 1, at]
            out[u : u + 1, count : 2 * count] = q[:, at]
    local[2:3] = jnp.broadcast_to(
        jnp.sum(rows[:1] * rows[:1], axis=1, keepdims=True), (1, local.shape[1])
    )


def send_kernel(local, remote, *refs):
    *outs, table = refs
    table[0:2] = local[0:2]
    table[2:4] = remote[0:2]
    mine = lax.axis_index("ex") ^ lax.axis_index("col")
    for step, out in enumerate(outs):
        out[...] = jnp.concatenate(
            [table[pl.ds(mine ^ step, 1), :], local[2:8], local[7:8]], axis=0
        )


def last_kernel(all_cols, m, k, own, *refs):
    parts, (features, scores) = refs[:-2], refs[-2:]
    total = parts[0][...]
    for part in parts[1:]:
        total = total + part[...]
    count = scores.shape[1]
    scale = lax.rsqrt(total[1:2, 0:1] / all_cols + epsilon)
    target_scale = lax.rsqrt(total[0:1, count : 2 * count] / all_cols + epsilon)
    scores[...] = total[0:1, 0:count] * scale * target_scale / math.sqrt(all_cols)
    block = own[...] * scale
    for r, at in enumerate(column_starts(m, k, block.shape[0])):
        features[:, at : at + LANES] = block[r : r + 1]


def call(kernel, out_shape, in_specs, name, limit, scratch=(), flops=0, moved=0):
    single = not isinstance(out_shape, list)
    return pl.pallas_call(
        kernel,
        out_shape=out_shape,
        in_specs=in_specs,
        out_specs=VMEM if single else [VMEM] * len(out_shape),
        scratch_shapes=scratch,
        compiler_params=pltpu.CompilerParams(vmem_limit_bytes=limit * MIB),
        cost_estimate=pl.CostEstimate(flops=flops, bytes_accessed=moved, transcendentals=0),
        name=name,
    )


def on_device(
    hidden_input,
    output_gradient,
    lengths,
    adapter_down,
    adapter_up,
    left_sign_words,
    right_sign_words,
    targets,
    *,
    exs,
    cols,
):
    _, layers, seq, width = hidden_input.shape
    m = right_sign_words.shape[3]
    rank = adapter_down.shape[1]
    k = left_sign_words.shape[2] * WORD
    count, own_cols = targets.shape
    all_cols = own_cols * cols
    right = jnp.swapaxes(right_sign_words, 2, 3)
    neighbours = shift(targets, "ex", exs, 1)
    rows = jax.ShapeDtypeStruct(hidden_input.shape, bf16)
    mixed, hidden, grad = call(
        mix_kernel,
        [jax.ShapeDtypeStruct((layers * 2 * m, seq), f32), rows, rows],
        [HBM] * 5,
        "mix",
        8,
        [
            pltpu.VMEM(right.shape, jnp.int32),
            pltpu.VMEM((layers, rank, width), bf16),
            pltpu.VMEM((layers, width, rank), bf16),
            pltpu.SemaphoreType.DMA((4 * layers + 1,)),
        ],
        4 * layers * seq * width * rank,
        4 * MIB,
    )(*in_hbm(right, hidden_input, output_gradient, adapter_down, adapter_up))
    others = [shift(mixed, "col", cols, s) for s in range(cols - 1, 0, -1)]
    signed = jax.ShapeDtypeStruct((layers, 2, seq, k), bf16)
    high, low = call(
        sign_kernel,
        [signed, signed],
        [VMEM] * 3,
        "sign",
        8,
        [pltpu.VMEM((2, k, width), bf16)],
        4 * layers * k * seq * width,
        6 * MIB,
    )(left_sign_words, hidden, grad)

    def split(*tables):
        size = count * len(tables)
        return call(
            split_kernel,
            [
                jax.ShapeDtypeStruct((own_cols, 2 * size), bf16),
                jax.ShapeDtypeStruct((1, size), f32),
            ],
            [VMEM] * len(tables),
            "split",
            8,
            moved=MIB,
        )(*tables)

    block = (own_cols // LANES, LANES)
    lanes = -(-2 * count // LANES) * LANES
    shape = jax.ShapeDtypeStruct(block, f32)
    packed = jax.ShapeDtypeStruct((2 * exs, lanes), f32)
    results = [
        jax.ShapeDtypeStruct((1, own_cols), f32),
        jax.ShapeDtypeStruct((1, count * exs // cols), f32),
    ]
    inputs = (lengths.reshape(1, 1), mixed, *others, high, low)
    last = functools.partial(last_kernel, all_cols, m, k)
    if exs == 4 and cols == 4:
        blocks = call(
            functools.partial(pair_kernel, cols),
            [jax.ShapeDtypeStruct((2,) + block, f32)] * cols,
            [VMEM] * len(inputs),
            "sketch",
            8,
            [pltpu.VMEM((cols,) + block, f32)],
        )(*inputs)
        received = [shift(blocks[s], "col", cols, s) for s in STEPS]
        own, pair = call(sum_kernel, [shape] * 2, [VMEM] * cols, "own", 2)(blocks[0], *received)
        other = crossed(pair, exs, cols)
        line = jax.ShapeDtypeStruct((8, lanes), f32)
        local, remote = call(
            functools.partial(paired_kernel, m, k), [line, line], [VMEM] * 4, "score", 8
        )(own, other, *split(targets, neighbours))
        lines = call(
            send_kernel, [line] * cols, [VMEM] * 2, "send", 2, [pltpu.VMEM((4, lanes), f32)]
        )(local, crossed(remote, exs, cols))
        parts = [lines[0]] + [shift(lines[s], "col", cols, s) for s in STEPS]
        return tuple(
            call(last, results, [VMEM] * (1 + len(parts)), "last", 2)(own, *parts)
        )
    blocks = call(
        functools.partial(spread_kernel, exs, cols),
        jax.ShapeDtypeStruct((exs * cols,) + block, f32),
        [VMEM] * len(inputs),
        "sketch",
        8,
    )(*inputs)
    received = lax.all_to_all(blocks, ("ex", "col"), 0, 0, tiled=True)
    own, packed = call(
        functools.partial(gathered_kernel, exs, cols, m, k), [shape, packed], [VMEM] * 3, "score", 16
    )(received, *split(targets))
    per = exs // cols
    rows = jnp.stack([packed[:exs], packed[exs:]], axis=1)
    grid = jnp.zeros((exs, cols) + rows.shape[1:], f32)
    grid = grid.at[:, lax.axis_index("ex") // per].set(rows)
    back = lax.all_to_all(
        grid.reshape((exs * cols,) + rows.shape[1:]), ("ex", "col"), 0, 0, tiled=True
    ).reshape((exs, cols) + rows.shape[1:])
    mine = lax.dynamic_slice_in_dim(back, lax.axis_index("col") * per, per, axis=0).sum(axis=1)
    total = jnp.concatenate(
        [
            jnp.concatenate([mine[:, 0, :count].reshape(1, -1), mine[:, 0, count : 2 * count].reshape(1, -1)], axis=1),
            jnp.broadcast_to(mine[:1, 1, :1], (1, 2 * count * per)),
        ],
        axis=0,
    )
    return tuple(
        call(last, results, [VMEM] * 2, "last", 2)(own, total)
    )


def solution(mesh):
    body = functools.partial(on_device, exs=mesh.shape["ex"], cols=mesh.shape["col"])
    return jax.shard_map(
        body,
        mesh=mesh,
        in_specs=(
            P(("grp", "ex"), None, None, "col"),
            P(("grp", "ex"), None, None, "col"),
            P(("grp", "ex")),
            P(None, None, "col"),
            P(None, "col", None),
            P(None, None, None, "col"),
            P(),
            P(("grp", "ex"), "col"),
        ),
        out_specs=(P(("grp", "ex"), "col"), P(("grp", "ex"), "col")),
        check_vma=False,
    )
```

```python
import functools
import math

import jax
import jax.numpy as jnp
from jax import lax
from jax.experimental import pallas as pl
from jax.experimental.pallas import tpu as pltpu
from jax.sharding import PartitionSpec as P

epsilon = 1e-06
WORD = 16
STEPS = (1, 2, 3)
LANES = 128
f32, bf16 = jnp.float32, jnp.bfloat16
MIB = 1 << 20

def crossed(x, exs, cols):
    pairs = [(e * cols + i, (e ^ 2) * cols + (i ^ 1)) for e in range(exs) for i in range(cols)]
    return lax.ppermute(x, ("ex", "col"), pairs)


VMEM = pl.BlockSpec(memory_space=pltpu.VMEM)
HBM = pl.BlockSpec(memory_space=pltpu.HBM)


def contract_last(a, b):
    return lax.dot_general(a, b, (((1,), (1,)), ((), ())), preferred_element_type=f32)


def product(a, b):
    return jnp.dot(a, b, preferred_element_type=f32)


def halves(x):
    high = x.astype(bf16)
    return high, (x - high.astype(f32)).astype(bf16)


def partner(i, step, count):
    return i ^ step if count & (count - 1) == 0 else (i + step) % count


def shift(x, axis, count, step):
    return lax.ppermute(x, axis, [(i, partner(i, step, count)) for i in range(count)])


def in_hbm(*arrays):
    return [pltpu.with_memory_space_constraint(x, pltpu.HBM) for x in arrays]


def mix_kernel(
    right, hidden, grad, down, up, out, hid_out, grad_out, right_buf, down_buf, up_buf, sems
):
    layers = hidden.shape[1]
    sides = [(l, j) for l in range(layers) for j in range(2)]
    first = [(right, right_buf)]
    first += [((up if j else down).at[l], (up_buf if j else down_buf).at[l]) for l, j in sides]
    rows = [
        ((grad if j else hidden).at[0, l], (grad_out if j else hid_out).at[0, l]) for l, j in sides
    ]
    copies = [pltpu.make_async_copy(a, b, sems.at[i]) for i, (a, b) in enumerate(first + rows)]
    for copy in copies:
        copy.start()
    for copy in copies[: len(first)]:
        copy.wait()
    pairs = []
    for l, j in sides:
        signs = (2 * right_buf[l, j] - 1).astype(f32).astype(bf16)
        if j == 0:
            folded = product(signs, down_buf[l])
        else:
            folded = contract_last(signs, up_buf[l])
        pairs.append(jnp.concatenate(halves(folded), axis=0))
    for copy in copies[len(first) :]:
        copy.wait()
    for at, (l, j) in enumerate(sides):
        both = contract_last(pairs[at], (grad_out if j else hid_out)[0, l])
        m = both.shape[0] // 2
        out[at * m : (at + 1) * m, :] = both[:m] + both[m:]


def unpack(words, l, j, out):
    bits = 1 << lax.broadcasted_iota(jnp.int32, (WORD, 1), 0)
    width = words.shape[3]
    for w in range(words.shape[2]):
        word = jnp.broadcast_to(words[l, j, w : w + 1, :], (WORD, width))
        signs = jnp.where((word & bits) != 0, 1.0, -1.0)
        out[w * WORD : (w + 1) * WORD, :] = signs.astype(f32).astype(bf16)


def split_kernel(*refs):
    *targets, table, squares = refs
    t = jnp.concatenate([ref[...] for ref in targets], axis=0)
    turned = jnp.transpose(t)
    count = turned.shape[1]
    table[:, :count], table[:, count:] = halves(turned)
    squares[...] = jnp.sum(turned * turned, axis=0, keepdims=True)


def sign_kernel(words, hidden, grad, high, low, signs):
    items = [(l, j) for l in range(hidden.shape[1]) for j in range(2)]
    unpack(words, *items[0], signs.at[0])
    for i, (l, j) in enumerate(items):
        if i + 1 < len(items):
            unpack(words, *items[i + 1], signs.at[(i + 1) % 2])
        signed = contract_last((grad if j == 0 else hidden)[0, l], signs[i % 2])
        high[l, j], low[l, j] = halves(signed)


def sketch_blocks(cols, length, own, others, high, low):
    mixed = own[...]
    for other in others:
        mixed = mixed + other[...]
    n = length[...]
    positions = lax.broadcasted_iota(jnp.int32, (1, mixed.shape[1]), 1)
    mixed = mixed * jnp.where(positions < n, 1.0 / n.astype(f32), 0.0)
    layers, sides, _, k = high.shape
    m = mixed.shape[0] // (layers * sides)
    pieces = []
    for l in range(layers):
        for j in range(sides):
            base = (2 * l + j) * m
            pair = jnp.concatenate(halves(mixed[base : base + m]), axis=0)
            both = product(pair, high[l, j]) + product(pair, low[l, j])
            both = both[:m] + both[m:]
            pieces += [both[:, q : q + LANES] for q in range(0, k, LANES)]
    per = len(pieces) // cols
    return [jnp.concatenate(pieces[i * per : (i + 1) * per], axis=0) for i in range(cols)]


def spread_kernel(exs, cols, length, own, *refs):
    others, (high, low, out) = refs[: cols - 1], refs[cols - 1 :]
    for i, block in enumerate(sketch_blocks(cols, length, own, others, high, low)):
        for e in range(exs):
            out[e * cols + i] = block


def pair_kernel(cols, length, own, *refs):
    others, (high, low), outs = refs[: cols - 1], refs[cols - 1 : cols + 1], refs[cols + 1 :]
    blocks = sketch_blocks(cols, length, own, others, high, low)
    me = lax.axis_index("col")

    def pick(at):
        low_pair = [jnp.where(at & 1 == 0, blocks[i], blocks[i + 1]) for i in (0, 2)]
        return jnp.where(at & 2 == 0, *low_pair)

    for step, out in enumerate(outs):
        to = partner(me, step, cols)
        out[0] = pick(to)
        out[1] = pick(to ^ 1)


def sum_kernel(*refs):
    *parts, own, pair = refs
    total = sum(part[...] for part in parts)
    own[...] = total[0]
    pair[...] = total[1]


def column_starts(m, k, count):
    per = k // LANES
    return [
        (r // (m * per)) * m * k + (r % m) * k + (r // m % per) * LANES for r in range(count)
    ]


def score(total, m, k, table, squares, out):
    exs = total.shape[0]
    starts = column_starts(m, k, total.shape[1])
    order = sorted(range(len(starts)), key=lambda r: starts[r])
    rows = jnp.concatenate([total[:, r, :] for r in order], axis=1)
    pair = jnp.concatenate(halves(rows), axis=0)
    both = product(pair, table[...])
    count = squares.shape[1]
    both = both[:, :count] + both[:, count:]
    out[...] = jnp.zeros_like(out)
    out[0:exs, 0:count] = both[:exs] + both[exs:]
    out[0:exs, count : 2 * count] = jnp.broadcast_to(squares[...], (exs, count))
    out[exs : 2 * exs, :] = jnp.broadcast_to(
        jnp.sum(rows * rows, axis=1, keepdims=True), (exs, out.shape[1])
    )


def gathered_kernel(exs, cols, m, k, received, table, squares, own, out):
    def collect(x):
        total = x[:, 0]
        for i in range(1, cols):
            total = total + x[:, i]
        return total

    x = received[...]
    score(
        collect(x.reshape((exs, cols) + x.shape[1:])), m, k, table, squares, out
    )
    mine = received[pl.ds(lax.axis_index("ex") * cols, cols)]
    own[...] = collect(mine[None])[0]


def paired_kernel(m, k, own, other, table, squares, local, remote):
    blocks = jnp.concatenate([own[...][None], other[...][None]], axis=0)
    starts = column_starts(m, k, blocks.shape[1])
    order = sorted(range(len(starts)), key=lambda r: starts[r])
    rows = jnp.concatenate([blocks[:, r, :] for r in order], axis=1)
    pair = jnp.concatenate(halves(rows), axis=0)
    both = product(pair, table[...])
    both = both[:2] + both[2:]
    total = squares.shape[1]
    both = both[:, :total] + both[:, total:]
    count = total // 2
    q = squares[...]
    for out, row in ((local, 0), (remote, 1)):
        out[...] = jnp.zeros_like(out)
        for u in range(2):
            at = slice(u * count, (u + 1) * count)
            out[u : u + 1, 0:count] = both[row : row + 1, at]
            out[u : u + 1, count : 2 * count] = q[:, at]
    local[2:3] = jnp.broadcast_to(
        jnp.sum(rows[:1] * rows[:1], axis=1, keepdims=True), (1, local.shape[1])
    )


def send_kernel(local, remote, *refs):
    *outs, table = refs
    table[0:2] = local[0:2]
    table[2:4] = remote[0:2]
    mine = lax.axis_index("ex") ^ lax.axis_index("col")
    for step, out in enumerate(outs):
        out[...] = jnp.concatenate(
            [table[pl.ds(mine ^ step, 1), :], local[2:8], local[7:8]], axis=0
        )


def last_kernel(all_cols, m, k, own, *refs):
    parts, (features, scores) = refs[:-2], refs[-2:]
    total = parts[0][...]
    for part in parts[1:]:
        total = total + part[...]
    count = scores.shape[1]
    scale = lax.rsqrt(total[1:2, 0:1] / all_cols + epsilon)
    target_scale = lax.rsqrt(total[0:1, count : 2 * count] / all_cols + epsilon)
    scores[...] = total[0:1, 0:count] * scale * target_scale / math.sqrt(all_cols)
    block = own[...] * scale
    for r, at in enumerate(column_starts(m, k, block.shape[0])):
        features[:, at : at + LANES] = block[r : r + 1]


def call(kernel, out_shape, in_specs, name, limit, scratch=(), flops=0, moved=0):
    single = not isinstance(out_shape, list)
    return pl.pallas_call(
        kernel,
        out_shape=out_shape,
        in_specs=in_specs,
        out_specs=VMEM if single else [VMEM] * len(out_shape),
        scratch_shapes=scratch,
        compiler_params=pltpu.CompilerParams(vmem_limit_bytes=limit * MIB),
        cost_estimate=pl.CostEstimate(flops=flops, bytes_accessed=moved, transcendentals=0),
        name=name,
    )


def on_device(
    hidden_input,
    output_gradient,
    lengths,
    adapter_down,
    adapter_up,
    left_sign_words,
    right_sign_words,
    targets,
    *,
    exs,
    cols,
):
    _, layers, seq, width = hidden_input.shape
    m = right_sign_words.shape[3]
    rank = adapter_down.shape[1]
    k = left_sign_words.shape[2] * WORD
    count, own_cols = targets.shape
    all_cols = own_cols * cols
    right = jnp.swapaxes(right_sign_words, 2, 3)
    neighbours = shift(targets, "ex", exs, 1)
    rows = jax.ShapeDtypeStruct(hidden_input.shape, bf16)
    mixed, hidden, grad = call(
        mix_kernel,
        [jax.ShapeDtypeStruct((layers * 2 * m, seq), f32), rows, rows],
        [HBM] * 5,
        "mix",
        8,
        [
            pltpu.VMEM(right.shape, jnp.int32),
            pltpu.VMEM((layers, rank, width), bf16),
            pltpu.VMEM((layers, width, rank), bf16),
            pltpu.SemaphoreType.DMA((4 * layers + 1,)),
        ],
        4 * layers * seq * width * rank,
        4 * MIB,
    )(*in_hbm(right, hidden_input, output_gradient, adapter_down, adapter_up))
    others = [shift(mixed, "col", cols, s) for s in range(cols - 1, 0, -1)]
    signed = jax.ShapeDtypeStruct((layers, 2, seq, k), bf16)
    high, low = call(
        sign_kernel,
        [signed, signed],
        [VMEM] * 3,
        "sign",
        8,
        [pltpu.VMEM((2, k, width), bf16)],
        4 * layers * k * seq * width,
        6 * MIB,
    )(left_sign_words, hidden, grad)

    def split(*tables):
        size = count * len(tables)
        return call(
            split_kernel,
            [
                jax.ShapeDtypeStruct((own_cols, 2 * size), bf16),
                jax.ShapeDtypeStruct((1, size), f32),
            ],
            [VMEM] * len(tables),
            "split",
            8,
            moved=MIB,
        )(*tables)

    block = (own_cols // LANES, LANES)
    lanes = -(-2 * count // LANES) * LANES
    shape = jax.ShapeDtypeStruct(block, f32)
    packed = jax.ShapeDtypeStruct((2 * exs, lanes), f32)
    results = [
        jax.ShapeDtypeStruct((1, own_cols), f32),
        jax.ShapeDtypeStruct((1, count * exs // cols), f32),
    ]
    inputs = (lengths.reshape(1, 1), mixed, *others, high, low)
    last = functools.partial(last_kernel, all_cols, m, k)
    if exs == 4 and cols == 4:
        blocks = call(
            functools.partial(pair_kernel, cols),
            [jax.ShapeDtypeStruct((2,) + block, f32)] * cols,
            [VMEM] * len(inputs),
            "sketch",
            8,
        )(*inputs)
        received = [shift(blocks[s], "col", cols, s) for s in (2, 3, 1)]
        own, pair = call(sum_kernel, [shape] * 2, [VMEM] * cols, "own", 2)(blocks[0], *received)
        other = crossed(pair, exs, cols)
        line = jax.ShapeDtypeStruct((8, lanes), f32)
        local, remote = call(
            functools.partial(paired_kernel, m, k), [line, line], [VMEM] * 4, "score", 8
        )(own, other, *split(targets, neighbours))
        lines = call(
            send_kernel, [line] * cols, [VMEM] * 2, "send", 2, [pltpu.VMEM((4, lanes), f32)]
        )(local, crossed(remote, exs, cols))
        parts = [lines[0]] + [shift(lines[s], "col", cols, s) for s in STEPS]
        return tuple(
            call(last, results, [VMEM] * (1 + len(parts)), "last", 2)(own, *parts)
        )
    blocks = call(
        functools.partial(spread_kernel, exs, cols),
        jax.ShapeDtypeStruct((exs * cols,) + block, f32),
        [VMEM] * len(inputs),
        "sketch",
        8,
    )(*inputs)
    received = lax.all_to_all(blocks, ("ex", "col"), 0, 0, tiled=True)
    own, packed = call(
        functools.partial(gathered_kernel, exs, cols, m, k), [shape, packed], [VMEM] * 3, "score", 16
    )(received, *split(targets))
    per = exs // cols
    rows = jnp.stack([packed[:exs], packed[exs:]], axis=1)
    grid = jnp.zeros((exs, cols) + rows.shape[1:], f32)
    grid = grid.at[:, lax.axis_index("ex") // per].set(rows)
    back = lax.all_to_all(
        grid.reshape((exs * cols,) + rows.shape[1:]), ("ex", "col"), 0, 0, tiled=True
    ).reshape((exs, cols) + rows.shape[1:])
    mine = lax.dynamic_slice_in_dim(back, lax.axis_index("col") * per, per, axis=0).sum(axis=1)
    total = jnp.concatenate(
        [
            jnp.concatenate([mine[:, 0, :count].reshape(1, -1), mine[:, 0, count : 2 * count].reshape(1, -1)], axis=1),
            jnp.broadcast_to(mine[:1, 1, :1], (1, 2 * count * per)),
        ],
        axis=0,
    )
    return tuple(
        call(last, results, [VMEM] * 2, "last", 2)(own, total)
    )


def solution(mesh):
    body = functools.partial(on_device, exs=mesh.shape["ex"], cols=mesh.shape["col"])
    return jax.shard_map(
        body,
        mesh=mesh,
        in_specs=(
            P(("grp", "ex"), None, None, "col"),
            P(("grp", "ex"), None, None, "col"),
            P(("grp", "ex")),
            P(None, None, "col"),
            P(None, "col", None),
            P(None, None, None, "col"),
            P(),
            P(("grp", "ex"), "col"),
        ),
        out_specs=(P(("grp", "ex"), "col"), P(("grp", "ex"), "col")),
        check_vma=False,
    )
```

```python
import functools
import math

import jax
import jax.numpy as jnp
from jax import lax
from jax.experimental import pallas as pl
from jax.experimental.pallas import tpu as pltpu
from jax.sharding import PartitionSpec as P

epsilon = 1e-06
WORD = 16
STEPS = (1, 2, 3)
LANES = 128
f32, bf16 = jnp.float32, jnp.bfloat16
MIB = 1 << 20

def crossed(x, exs, cols):
    pairs = [(e * cols + i, (e ^ 2) * cols + (i ^ 1)) for e in range(exs) for i in range(cols)]
    return lax.ppermute(x, ("ex", "col"), pairs)


VMEM = pl.BlockSpec(memory_space=pltpu.VMEM)
HBM = pl.BlockSpec(memory_space=pltpu.HBM)


def contract_last(a, b):
    return lax.dot_general(a, b, (((1,), (1,)), ((), ())), preferred_element_type=f32)


def product(a, b):
    return jnp.dot(a, b, preferred_element_type=f32)


def halves(x):
    high = x.astype(bf16)
    return high, (x - high.astype(f32)).astype(bf16)


def partner(i, step, count):
    return i ^ step if count & (count - 1) == 0 else (i + step) % count


def shift(x, axis, count, step):
    return lax.ppermute(x, axis, [(i, partner(i, step, count)) for i in range(count)])


def in_hbm(*arrays):
    return [pltpu.with_memory_space_constraint(x, pltpu.HBM) for x in arrays]


def mix_kernel(
    right, hidden, grad, down, up, out, hid_out, grad_out, right_buf, down_buf, up_buf, sems
):
    layers = hidden.shape[1]
    sides = [(l, j) for l in range(layers) for j in range(2)]
    first = [(right, right_buf)]
    first += [((up if j else down).at[l], (up_buf if j else down_buf).at[l]) for l, j in sides]
    rows = [
        ((grad if j else hidden).at[0, l], (grad_out if j else hid_out).at[0, l]) for l, j in sides
    ]
    copies = [pltpu.make_async_copy(a, b, sems.at[i]) for i, (a, b) in enumerate(first + rows)]
    for copy in copies:
        copy.start()
    for copy in copies[: len(first)]:
        copy.wait()
    pairs = []
    for l, j in sides:
        signs = (2 * right_buf[l, j] - 1).astype(f32).astype(bf16)
        if j == 0:
            folded = product(signs, down_buf[l])
        else:
            folded = contract_last(signs, up_buf[l])
        pairs.append(jnp.concatenate(halves(folded), axis=0))
    for copy in copies[len(first) :]:
        copy.wait()
    for at, (l, j) in enumerate(sides):
        both = contract_last(pairs[at], (grad_out if j else hid_out)[0, l])
        m = both.shape[0] // 2
        out[at * m : (at + 1) * m, :] = both[:m] + both[m:]


def unpack(words, l, j, out):
    bits = 1 << lax.broadcasted_iota(jnp.int32, (WORD, 1), 0)
    width = words.shape[3]
    for w in range(words.shape[2]):
        word = jnp.broadcast_to(words[l, j, w : w + 1, :], (WORD, width))
        signs = jnp.where((word & bits) != 0, 1.0, -1.0)
        out[w * WORD : (w + 1) * WORD, :] = signs.astype(f32).astype(bf16)


def split_kernel(*refs):
    *targets, table, squares = refs
    t = jnp.concatenate([ref[...] for ref in targets], axis=0)
    turned = jnp.transpose(t)
    count = turned.shape[1]
    table[:, :count], table[:, count:] = halves(turned)
    squares[...] = jnp.sum(turned * turned, axis=0, keepdims=True)


def sign_kernel(words, hidden, grad, high, low, signs):
    items = [(l, j) for l in range(hidden.shape[1]) for j in range(2)]
    unpack(words, *items[0], signs.at[0])
    for i, (l, j) in enumerate(items):
        if i + 1 < len(items):
            unpack(words, *items[i + 1], signs.at[(i + 1) % 2])
        signed = contract_last((grad if j == 0 else hidden)[0, l], signs[i % 2])
        high[l, j], low[l, j] = halves(signed)


def sketch_blocks(cols, length, own, others, high, low):
    mixed = own[...]
    for other in others:
        mixed = mixed + other[...]
    n = length[...]
    positions = lax.broadcasted_iota(jnp.int32, (1, mixed.shape[1]), 1)
    mixed = mixed * jnp.where(positions < n, 1.0 / n.astype(f32), 0.0)
    layers, sides, _, k = high.shape
    m = mixed.shape[0] // (layers * sides)
    pieces = []
    for l in range(layers):
        for j in range(sides):
            base = (2 * l + j) * m
            pair = jnp.concatenate(halves(mixed[base : base + m]), axis=0)
            both = product(pair, high[l, j]) + product(pair, low[l, j])
            both = both[:m] + both[m:]
            pieces += [both[:, q : q + LANES] for q in range(0, k, LANES)]
    per = len(pieces) // cols
    return [jnp.concatenate(pieces[i * per : (i + 1) * per], axis=0) for i in range(cols)]


def spread_kernel(exs, cols, length, own, *refs):
    others, (high, low, out) = refs[: cols - 1], refs[cols - 1 :]
    for i, block in enumerate(sketch_blocks(cols, length, own, others, high, low)):
        for e in range(exs):
            out[e * cols + i] = block


def pair_kernel(cols, length, own, *refs):
    others, (high, low), outs = refs[: cols - 1], refs[cols - 1 : cols + 1], refs[cols + 1 :]
    blocks = sketch_blocks(cols, length, own, others, high, low)
    me = lax.axis_index("col")

    def pick(at):
        low_pair = [jnp.where(at & 1 == 0, blocks[i], blocks[i + 1]) for i in (0, 2)]
        return jnp.where(at & 2 == 0, *low_pair)

    for step, out in enumerate(outs):
        to = partner(me, step, cols)
        out[0] = pick(to)
        out[1] = pick(to ^ 1)


def sum_kernel(*refs):
    *parts, own, pair = refs
    total = sum(part[...] for part in parts)
    own[...] = total[0]
    pair[...] = total[1]


def column_starts(m, k, count):
    per = k // LANES
    return [
        (r // (m * per)) * m * k + (r % m) * k + (r // m % per) * LANES for r in range(count)
    ]


def score(total, m, k, table, squares, out):
    exs = total.shape[0]
    starts = column_starts(m, k, total.shape[1])
    order = sorted(range(len(starts)), key=lambda r: starts[r])
    rows = jnp.concatenate([total[:, r, :] for r in order], axis=1)
    pair = jnp.concatenate(halves(rows), axis=0)
    both = product(pair, table[...])
    count = squares.shape[1]
    both = both[:, :count] + both[:, count:]
    out[...] = jnp.zeros_like(out)
    out[0:exs, 0:count] = both[:exs] + both[exs:]
    out[0:exs, count : 2 * count] = jnp.broadcast_to(squares[...], (exs, count))
    out[exs : 2 * exs, :] = jnp.broadcast_to(
        jnp.sum(rows * rows, axis=1, keepdims=True), (exs, out.shape[1])
    )


def gathered_kernel(exs, cols, m, k, received, table, squares, own, out):
    def collect(x):
        total = x[:, 0]
        for i in range(1, cols):
            total = total + x[:, i]
        return total

    x = received[...]
    score(
        collect(x.reshape((exs, cols) + x.shape[1:])), m, k, table, squares, out
    )
    mine = received[pl.ds(lax.axis_index("ex") * cols, cols)]
    own[...] = collect(mine[None])[0]


def paired_kernel(m, k, own, other, table, squares, local, remote):
    blocks = jnp.concatenate([own[...][None], other[...][None]], axis=0)
    starts = column_starts(m, k, blocks.shape[1])
    order = sorted(range(len(starts)), key=lambda r: starts[r])
    rows = jnp.concatenate([blocks[:, r, :] for r in order], axis=1)
    pair = jnp.concatenate(halves(rows), axis=0)
    both = product(pair, table[...])
    both = both[:2] + both[2:]
    total = squares.shape[1]
    both = both[:, :total] + both[:, total:]
    count = total // 2
    q = squares[...]
    for out, row in ((local, 0), (remote, 1)):
        out[...] = jnp.zeros_like(out)
        for u in range(2):
            at = slice(u * count, (u + 1) * count)
            out[u : u + 1, 0:count] = both[row : row + 1, at]
            out[u : u + 1, count : 2 * count] = q[:, at]
    local[2:3] = jnp.broadcast_to(
        jnp.sum(rows[:1] * rows[:1], axis=1, keepdims=True), (1, local.shape[1])
    )


def send_kernel(local, remote, *refs):
    *outs, table = refs
    table[0:2] = local[0:2]
    table[2:4] = remote[0:2]
    mine = lax.axis_index("ex") ^ lax.axis_index("col")
    for step, out in enumerate(outs):
        out[...] = jnp.concatenate(
            [table[pl.ds(mine ^ step, 1), :], local[2:8], local[7:8]], axis=0
        )


def last_kernel(all_cols, m, k, own, *refs):
    parts, (features, scores) = refs[:-2], refs[-2:]
    total = parts[0][...]
    for part in parts[1:]:
        total = total + part[...]
    count = scores.shape[1]
    scale = lax.rsqrt(total[1:2, 0:1] / all_cols + epsilon)
    target_scale = lax.rsqrt(total[0:1, count : 2 * count] / all_cols + epsilon)
    scores[...] = total[0:1, 0:count] * scale * target_scale / math.sqrt(all_cols)
    block = own[...] * scale
    for r, at in enumerate(column_starts(m, k, block.shape[0])):
        features[:, at : at + LANES] = block[r : r + 1]


def call(kernel, out_shape, in_specs, name, limit, scratch=(), flops=0, moved=0):
    single = not isinstance(out_shape, list)
    return pl.pallas_call(
        kernel,
        out_shape=out_shape,
        in_specs=in_specs,
        out_specs=VMEM if single else [VMEM] * len(out_shape),
        scratch_shapes=scratch,
        compiler_params=pltpu.CompilerParams(vmem_limit_bytes=limit * MIB),
        cost_estimate=pl.CostEstimate(flops=flops, bytes_accessed=moved, transcendentals=0),
        name=name,
    )


def on_device(
    hidden_input,
    output_gradient,
    lengths,
    adapter_down,
    adapter_up,
    left_sign_words,
    right_sign_words,
    targets,
    *,
    exs,
    cols,
):
    _, layers, seq, width = hidden_input.shape
    m = right_sign_words.shape[3]
    rank = adapter_down.shape[1]
    k = left_sign_words.shape[2] * WORD
    count, own_cols = targets.shape
    all_cols = own_cols * cols
    right = jnp.swapaxes(right_sign_words, 2, 3)
    neighbours = shift(targets, "ex", exs, 1)
    rows = jax.ShapeDtypeStruct(hidden_input.shape, bf16)
    mixed, hidden, grad = call(
        mix_kernel,
        [jax.ShapeDtypeStruct((layers * 2 * m, seq), f32), rows, rows],
        [HBM] * 5,
        "mix",
        8,
        [
            pltpu.VMEM(right.shape, jnp.int32),
            pltpu.VMEM((layers, rank, width), bf16),
            pltpu.VMEM((layers, width, rank), bf16),
            pltpu.SemaphoreType.DMA((4 * layers + 1,)),
        ],
        4 * layers * seq * width * rank,
        4 * MIB,
    )(*in_hbm(right, hidden_input, output_gradient, adapter_down, adapter_up))
    others = [shift(mixed, "col", cols, s) for s in range(cols - 1, 0, -1)]
    signed = jax.ShapeDtypeStruct((layers, 2, seq, k), bf16)
    high, low = call(
        sign_kernel,
        [signed, signed],
        [VMEM] * 3,
        "sign",
        8,
        [pltpu.VMEM((2, k, width), bf16)],
        4 * layers * k * seq * width,
        6 * MIB,
    )(left_sign_words, hidden, grad)

    def split(*tables):
        size = count * len(tables)
        return call(
            split_kernel,
            [
                jax.ShapeDtypeStruct((own_cols, 2 * size), bf16),
                jax.ShapeDtypeStruct((1, size), f32),
            ],
            [VMEM] * len(tables),
            "split",
            8,
            moved=MIB,
        )(*tables)

    block = (own_cols // LANES, LANES)
    lanes = -(-2 * count // LANES) * LANES
    shape = jax.ShapeDtypeStruct(block, f32)
    packed = jax.ShapeDtypeStruct((2 * exs, lanes), f32)
    results = [
        jax.ShapeDtypeStruct((1, own_cols), f32),
        jax.ShapeDtypeStruct((1, count * exs // cols), f32),
    ]
    inputs = (lengths.reshape(1, 1), mixed, *others, high, low)
    last = functools.partial(last_kernel, all_cols, m, k)
    if exs == 4 and cols == 4:
        blocks = call(
            functools.partial(pair_kernel, cols),
            [jax.ShapeDtypeStruct((2,) + block, f32)] * cols,
            [VMEM] * len(inputs),
            "sketch",
            8,
        )(*inputs)
        received = [shift(blocks[s], "col", cols, s) for s in STEPS]
        own, pair = call(sum_kernel, [shape] * 2, [VMEM] * cols, "own", 2)(blocks[0], *received)
        other = crossed(pair, exs, cols)
        line = jax.ShapeDtypeStruct((8, lanes), f32)
        local, remote = call(
            functools.partial(paired_kernel, m, k), [line, line], [VMEM] * 4, "score", 8
        )(own, other, *split(targets, neighbours))
        lines = call(
            send_kernel, [line] * cols, [VMEM] * 2, "send", 2, [pltpu.VMEM((4, lanes), f32)]
        )(local, crossed(remote, exs, cols))
        parts = [lines[0]] + [shift(lines[s], "col", cols, s) for s in STEPS]
        return tuple(
            call(last, results, [VMEM] * (1 + len(parts)), "last", 2)(own, *parts)
        )
    blocks = call(
        functools.partial(spread_kernel, exs, cols),
        jax.ShapeDtypeStruct((exs * cols,) + block, f32),
        [VMEM] * len(inputs),
        "sketch",
        8,
    )(*inputs)
    received = lax.all_to_all(blocks, ("ex", "col"), 0, 0, tiled=True)
    own, packed = call(
        functools.partial(gathered_kernel, exs, cols, m, k), [shape, packed], [VMEM] * 3, "score", 16
    )(received, *split(targets))
    per = exs // cols
    rows = jnp.stack([packed[:exs], packed[exs:]], axis=1)
    grid = jnp.zeros((exs, cols) + rows.shape[1:], f32)
    grid = grid.at[:, lax.axis_index("ex") // per].set(rows)
    back = lax.all_to_all(
        grid.reshape((exs * cols,) + rows.shape[1:]), ("ex", "col"), 0, 0, tiled=True
    ).reshape((exs, cols) + rows.shape[1:])
    mine = lax.dynamic_slice_in_dim(back, lax.axis_index("col") * per, per, axis=0).sum(axis=1)
    total = jnp.concatenate(
        [
            jnp.concatenate([mine[:, 0, :count].reshape(1, -1), mine[:, 0, count : 2 * count].reshape(1, -1)], axis=1),
            jnp.broadcast_to(mine[:1, 1, :1], (1, 2 * count * per)),
        ],
        axis=0,
    )
    return tuple(
        call(last, results, [VMEM] * 2, "last", 2)(own, total)
    )


def solution(mesh):
    body = functools.partial(on_device, exs=mesh.shape["ex"], cols=mesh.shape["col"])
    return jax.shard_map(
        body,
        mesh=mesh,
        in_specs=(
            P(("grp", "ex"), None, None, "col"),
            P(("grp", "ex"), None, None, "col"),
            P(("grp", "ex")),
            P(None, None, "col"),
            P(None, "col", None),
            P(None, None, None, "col"),
            P(),
            P(("grp", "ex"), "col"),
        ),
        out_specs=(P(("grp", "ex"), "col"), P(("grp", "ex"), "col")),
        check_vma=False,
    )
```
